256 devices in a mesh: obs: 4 (over x), pix: 16 (over z, core), chan: 4 (over y).
Axes of the slice: x: 4, y: 4, z: 8, core: 2. Of those that a mesh axis runs over, the one named last changes fastest.
Arguments:
- spectra: bfloat16 [131072, 4608], P(('obs', 'pix'), 'chan'), may hold values from -6 to 6
- enc_weight: bfloat16 [4608, 256], P('chan'), may hold values from -0.09375 to 0.09375
- pix_tile: int32 [131072, 1], P(('obs', 'pix')), may hold values from 0 to 15; in each aligned block of 512 rows (0 to 511, 512 to 1023, ...) at most 64 rows name the same one
- pix_local: int32 [131072], P(('obs', 'pix')), may hold values from 0 to 4095
- foot_weight: float32 [131072], P(('obs', 'pix')), may hold values from 0.001 to 0.01
- cotangent: bfloat16 [65536, 256], P('pix'), may hold values from -6 to 6
- adjoint: int32 [8, 65536], P(None, 'pix'), may hold values from 0 to 65535, as said below
- mixing: float32 [8, 256], replicated, may hold values from -2 to 2
Outputs:
- grad_enc: float32 [4608, 256], P('chan')
The draws below stay inside these ranges and needn't reach their ends.
Inputs may be any that keep to these rules, and one draw needn't show every extreme that they name: `pix_tile`: in each aligned block of 512 rows no tile is named by more than 64 rows, a bound that some block reaches. `adjoint`: every entry is a pixel at most 128 away in index from its column's pixel; in every column the first entry is exactly 128 away.
All inputs are finite; a program needn't handle non-finite values.
Results may differ from the reference program's by a relative error of at most 0.006.
Values may be sent and summed in bfloat16 or wider, within the bound.
A program may use at most 128 MiB of HBM per device.

```python
import math
import jax
import jax.numpy as jnp
import numpy as np
from jax import lax

CHANNELS = 4608
EMBED = 256
NEIGH = 8
HALO = 128
PT = 4096
QROWS = 512
CAP = 64
NTILES = 16
NPIX = 65536
FOOTPRINTS = 131072
N_CHAN = 4


def draw_adjoint(key, part):
    key_offset, key_sign = jax.random.split(jax.random.fold_in(key, 17))
    position = jnp.arange(NPIX, dtype=jnp.int32)
    offsets = jax.random.randint(key_offset, (NEIGH, NPIX), -HALO, HALO + 1).astype(jnp.int32)
    signs = (jax.random.randint(key_sign, (NPIX,), 0, 2) * 2 - 1).astype(jnp.int32)
    offsets = offsets.at[0].set(signs * HALO)
    candidate = position[None, :] + offsets
    inside = (candidate >= 0) & (candidate < NPIX)
    return jnp.where(inside, candidate, position[None, :] - offsets).astype(jnp.int32)


def touch_ends(array, rng, low, top_value):
    place = [jax.random.randint(jax.random.fold_in(rng, axis), (), 0, length) for axis, length in enumerate(array.shape)]
    widest = array.shape.index(max(array.shape))
    next_to = place[:widest] + [(place[widest] + 1) % array.shape[widest]] + place[widest + 1:]
    return array.at[tuple(place)].set(low).at[tuple(next_to)].set(top_value)


def level_of(own_key, shape, cuts, least, high):
    def one(dim, parts):
        draws = jax.random.uniform(jax.random.fold_in(jax.random.fold_in(own_key, 6), dim), (parts,), jnp.float32, least / len(cuts), high / len(cuts))
        return jnp.repeat(jnp.exp(draws), shape[dim] // parts).reshape((-1,) + (1,) * (len(shape) - dim - 1))

    gain = one(*cuts[0])
    for cut in cuts[1:]:
        gain = gain * one(*cut)
    return gain


def deal_out(own_key, own, number, rows, amount, top, most, lean):
    sequence = jax.random.permutation(own_key, amount)
    heavy_load, ordinary = load_shares(amount, rows * top, most, lean, True), load_shares(amount, rows * top, most, lean, False)
    places = jnp.arange(amount)

    def named(tallies, rotation):
        used = int((tallies > 0).sum())
        fixed = max(1, used // 4)
        moved = fixed + (places - fixed + rotation * (used - fixed)) % max(1, amount - fixed)
        return jnp.zeros((amount,), jnp.int32).at[sequence[jnp.where(places < fixed, places, moved)]].set(jnp.asarray(tallies, jnp.int32))

    tallies = jnp.where(number % 4 == 0, named(heavy_load, number // 4), named(ordinary, number - number // 4 - 1))
    mixed = jax.random.permutation(jax.random.fold_in(own, 3), amount)
    giver, receiver = mixed[0:amount // 2 * 2:2], mixed[1:amount // 2 * 2:2]
    slack = jnp.minimum(tallies[giver] - 1, most - tallies[receiver]) // 2
    slack = jnp.where((giver == sequence[0]) | (receiver == sequence[0]) | (tallies[receiver] == 0), 0, jnp.maximum(slack, 0))
    moved = jax.random.randint(jax.random.fold_in(own, 4), (amount // 2,), 0, 1 << 20) % (slack + 1)
    tallies = tallies.at[giver].add(-moved).at[receiver].add(moved)
    labels = jnp.searchsorted(jnp.cumsum(tallies), jnp.arange(rows * top), side="right").astype(jnp.int32)
    listing = labels.reshape(top, rows).T
    listing = listing[jax.random.permutation(jax.random.fold_in(own, 1), rows)]
    rotation = jax.random.randint(jax.random.fold_in(own, 2), (rows, 1), 0, top)
    return jnp.take_along_axis(listing, (jnp.arange(top)[None, :] + rotation) % top, axis=1)


def load_shares(number_of, total, bound, lean, full):
    loads = [(1 << 20) // math.isqrt(grade ** lean) + 1 for grade in range(1, number_of + 1)]
    largest = bound if full else min(bound, max(-(-total // number_of), total * loads[0] // sum(loads)))
    least = 1 if total - largest >= number_of - 1 else 0
    holding, surplus = [largest] + [least] * (number_of - 1), total - largest - least * (number_of - 1)
    while surplus > 0:
        free = [i for i in range(1, number_of) if holding[i] < largest] or [i for i in range(1, number_of) if holding[i] < bound]
        mass, budget = sum([loads[i] for i in free]), surplus
        for i in free:
            more = min(bound - holding[i], max(1, budget * loads[i] // mass), surplus)
            holding[i] = holding[i] + more
            surplus = surplus - more
    return np.array(holding)


def bell_draw(key, shape, width, bound, pieces=(), kind=jnp.bfloat16):
    values = width * jax.random.normal(key, shape, jnp.float32)
    if pieces:
        values = values * level_of(key, shape, pieces, -0.22, 0.18)
    return jnp.clip(values, -bound, bound).astype(kind)


def setup_inputs(seed: int = 0) -> dict:
    key_of = jax.random.split(jax.random.key(seed), 9)
    spectra = bell_draw(key_of[0], (FOOTPRINTS, CHANNELS), 1.0, 6.0, ((0, 64), (1, 4)))
    enc_weight = bell_draw(key_of[1], (CHANNELS, EMBED), CHANNELS ** -0.5, 0.09375, ((0, 4),))
    pix_tile_keys = jax.random.split(jax.random.fold_in(key_of[2], 1), FOOTPRINTS // QROWS)
    pix_tile_turns = jax.random.permutation(jax.random.fold_in(key_of[2], 3), FOOTPRINTS // QROWS)
    pix_tile = jax.vmap(lambda own, number: deal_out(jax.random.fold_in(key_of[2], 2), own, number, QROWS, NTILES, 1, CAP, 2))(pix_tile_keys, pix_tile_turns).reshape((FOOTPRINTS, 1))
    pix_local = touch_ends(jax.random.randint(key_of[3], (FOOTPRINTS,), 0, PT), jax.random.fold_in(key_of[3], 1), 0, PT - 1).astype(jnp.int32)
    foot_weight = jnp.clip(jnp.exp(math.log(0.01) - 2.30258502 * jax.random.uniform(key_of[4], (FOOTPRINTS,), jnp.float32) ** level_of(key_of[4], (FOOTPRINTS,), ((0, 64),), -0.2, 0.2)), 0.001, 0.01)
    cotangent = bell_draw(key_of[5], (NPIX, EMBED), 1.0, 6.0, ((0, 16),))
    adjoint = draw_adjoint(jax.random.fold_in(key_of[8], 71), 0)
    mixing = bell_draw(key_of[7], (NEIGH, EMBED), 0.35, 2.0, (), jnp.float32)
    return dict(spectra=spectra, enc_weight=enc_weight, pix_tile=pix_tile, pix_local=pix_local, foot_weight=foot_weight, cotangent=cotangent, adjoint=adjoint, mixing=mixing)


def reference(spectra, enc_weight, pix_tile, pix_local, foot_weight, cotangent, adjoint, mixing):
    group_width = CHANNELS // N_CHAN
    pre = jnp.zeros((spectra.shape[0], enc_weight.shape[1]), jnp.float32)
    for group in range(N_CHAN):
        lower = group * group_width
        partial_value = jnp.dot(spectra[:, lower:lower + group_width], enc_weight[lower:lower + group_width], preferred_element_type=jnp.float32)
        rounded = lax.optimization_barrier(partial_value.astype(jnp.bfloat16))
        pre = pre + rounded.astype(jnp.float32)
    sigma = jax.nn.sigmoid(pre)
    deriv = sigma * (1.0 + pre * (1.0 - sigma))
    summed = cotangent.astype(jnp.float32)
    for neighbor in range(NEIGH):
        summed = summed + jnp.take(cotangent, adjoint[neighbor], axis=0).astype(jnp.float32) * mixing[neighbor]
    pixel_grad = summed.astype(jnp.bfloat16)
    pixel_index = (pix_tile[:, 0] * PT + pix_local).astype(jnp.int32)
    fetched = jnp.take(pixel_grad, pixel_index, axis=0).astype(jnp.float32)
    grad_pre = (foot_weight[:, None] * deriv * fetched).astype(jnp.bfloat16)
    return lax.dot_general(spectra, grad_pre, (((0,), (0,)), ((), ())), preferred_element_type=jnp.float32)
```

```python
import jax
import jax.numpy as jnp
from jax import lax
from jax.experimental import pallas as pl
from jax.experimental.pallas import tpu as pltpu
from jax.sharding import Mesh
from jax.sharding import PartitionSpec as P

NEIGH = 8
HALO = 128
PIX = ("pix_0", "pix_1")
OBS_PIX = ("obs", "pix_0", "pix_1")
BF16 = jnp.bfloat16
F32 = jnp.float32


def extended(value, sides, width):
    for axis, dim in sides:
        size, length = (lax.axis_size(axis), value.shape[dim])
        up = [(i, (i + 1) % size) for i in range(size - 1)]
        down = [(j, i) for i, j in up]
        last = lax.slice_in_dim(value, length - width, length, axis=dim)
        first = lax.slice_in_dim(value, 0, width, axis=dim)
        before = lax.ppermute(last, axis, up)
        after = lax.ppermute(first, axis, down)
        value = jnp.concatenate([before, value, after], axis=dim)
    return value


def in_blocks(value, dim, length):
    before, after = (value.shape[:dim], value.shape[dim + 1 :])
    return jnp.moveaxis(value.reshape(*before, length, -1, *after), dim, 0)


def summed_on_arrival(value, axis, dim):
    pieces = in_blocks(value, dim, lax.axis_size(axis))
    arrived = lax.all_to_all(pieces, axis, split_axis=0, concat_axis=0, tiled=True)
    return arrived.astype(jnp.float32).sum(axis=0)


def fetch_rows(pixel_grad, tile_ids, local_ids, capacity):
    tile_count = lax.axis_size(PIX)
    feature_count = pixel_grad.shape[1]
    onehot = (tile_ids[:, None] == jnp.arange(tile_count, dtype=jnp.int32)[None, :]).astype(
        jnp.int32
    )
    place_rank = jnp.sum((jnp.cumsum(onehot, axis=0) - 1) * onehot, axis=1)
    slot_index = tile_ids * capacity + place_rank
    outgoing = jnp.full((tile_count * capacity,), -1, jnp.int32).at[slot_index].set(local_ids)
    outgoing = outgoing.reshape(tile_count, capacity)
    requested = lax.all_to_all(outgoing, PIX, split_axis=0, concat_axis=0, tiled=True)
    usable = requested >= 0
    fetched = jnp.take(pixel_grad, jnp.where(usable, requested, 0), axis=0)
    fetched = jnp.where(usable[..., None], fetched, jnp.zeros_like(fetched))
    answers = lax.all_to_all(fetched, PIX, split_axis=0, concat_axis=0, tiled=True)
    return jnp.take(answers.reshape(tile_count * capacity, feature_count), slot_index, axis=0)


def pre_gradient(pre, fetched, weights):
    sigma = jax.nn.sigmoid(pre)
    deriv = sigma * (1.0 + pre * (1.0 - sigma))
    return (weights[:, None] * deriv * fetched.astype(jnp.float32)).astype(jnp.bfloat16)


def send(source, target, send_sem, recv_sem, where):
    return pltpu.make_async_remote_copy(
        src_ref=source,
        dst_ref=target,
        send_sem=send_sem,
        recv_sem=recv_sem,
        device_id=where,
        device_id_type=pl.DeviceIdType.MESH,
    )


def greet(groups):
    barrier = pltpu.get_barrier_semaphore()
    count = 0
    for name, size in groups:
        me = lax.axis_index(name)
        for step in range(1, size):
            pl.semaphore_signal(
                barrier,
                inc=1,
                device_id={name: lax.rem(me + step, size)},
                device_id_type=pl.DeviceIdType.MESH,
            )
            count += 1
    pl.semaphore_wait(barrier, count)


def gather_multiply(part, spec, spec_copies, shards, total, gs, gr):
    y = lax.axis_index("chan")
    right, left, far = lax.rem(y + 1, 4), lax.rem(y + 3, 4), lax.rem(y + 2, 4)
    rows = part.shape[0]
    lo, hi = pl.ds(0, rows // 2), pl.ds(rows // 2, rows // 2)
    to_right, to_left = {"chan": right}, {"chan": left}
    sends = [
        send(part.at[lo], shards.at[y, lo], gs.at[0], gr.at[0], to_right),
        send(part.at[hi], shards.at[y, hi], gs.at[1], gr.at[1], to_left),
        send(part.at[hi], shards.at[y, hi], gs.at[2], gr.at[2], to_right),
        send(part.at[lo], shards.at[y, lo], gs.at[3], gr.at[3], to_left),
    ]
    for copy in sends:
        copy.start()

    width = total.shape[1] // 3

    def multiply(gradient, owner, step):
        spec_copies[step].wait()
        turned = jnp.transpose(gradient.astype(F32)).astype(BF16)
        for n in range(3):
            columns = pl.ds(n * width, width)
            block = spec[pl.ds(pl.multiple_of(owner * rows, rows), rows), columns]
            product = jnp.dot(turned, block, preferred_element_type=F32)
            if step:
                total[:, columns] += product
            else:
                total[:, columns] = product

    multiply(part[...], y, 0)
    send(part.at[lo], shards.at[left, lo], gs.at[0], gr.at[0], to_right).wait_recv()
    sends.append(send(shards.at[left, lo], shards.at[left, lo], gs.at[4], gr.at[4], to_right))
    sends[4].start()
    send(part.at[hi], shards.at[right, hi], gs.at[1], gr.at[1], to_left).wait_recv()
    sends.append(send(shards.at[right, hi], shards.at[right, hi], gs.at[5], gr.at[5], to_left))
    sends[5].start()
    send(part.at[hi], shards.at[left, hi], gs.at[2], gr.at[2], to_right).wait_recv()
    multiply(shards[left], left, 1)
    send(part.at[lo], shards.at[right, lo], gs.at[3], gr.at[3], to_left).wait_recv()
    multiply(shards[right], right, 2)
    send(part.at[lo], shards.at[far, lo], gs.at[4], gr.at[4], to_right).wait_recv()
    send(part.at[hi], shards.at[far, hi], gs.at[5], gr.at[5], to_left).wait_recv()
    multiply(shards[far], far, 3)
    return sends


def add_up(total, out, half_out, half_in, turned, xs, xr, zf, zs, zr, pieces, sems):
    core_s, core_r, xs_s, xs_r, zs_s, zs_r, pz_s, pz_r, px_s, px_r, pc_s, pc_r = sems
    x, z, c = (lax.axis_index(name) for name in ("obs", "pix_0", "pix_1"))
    o = 1 - c
    lines, wide = xs.shape[1], zf.shape[1]
    sends = []

    half_out[...] = total[pl.ds(pl.multiple_of(o * 128, 128), 128), :].astype(BF16)
    swap = send(half_out, half_in, core_s, core_r, {"pix_1": o})
    swap.start()
    sends.append(swap)
    swap.wait_recv()
    mine = pl.ds(pl.multiple_of(c * 128, 128), 128)
    for j in range(total.shape[1] // 128):
        block = pl.ds(j * 128, 128)
        turned[block, :] = jnp.transpose(total[mine, block] + half_in[:, block].astype(F32))

    for j in range(4):
        xs[j] = turned[pl.ds(j * lines, lines), :].astype(BF16)
    for d in (1, 3, 2):
        peer = lax.rem(x + d, 4)
        copy = send(xs.at[peer], xr.at[x], xs_s.at[d - 1], xs_r.at[d - 1], {"obs": peer})
        copy.start()
        sends.append(copy)
    summed = turned[pl.ds(pl.multiple_of(x * lines, 8), lines), :]
    for d in (1, 3, 2):
        origin = lax.rem(x + 4 - d, 4)
        send(xs.at[0], xr.at[origin], xs_s.at[d - 1], xs_r.at[d - 1], {"obs": origin}).wait_recv()
        summed = summed + xr[origin].astype(F32)
    turned[pl.ds(0, lines), :] = summed

    for j in range(8):
        zf[j] = turned[pl.ds(j * wide, wide), :]
        zs[j] = zf[j].astype(BF16)
    steps = (1, 7, 2, 6, 3, 5, 4)
    for d in steps:
        peer = lax.rem(z + d, 8)
        copy = send(zs.at[peer], zr.at[z], zs_s.at[d - 1], zs_r.at[d - 1], {"pix_0": peer})
        copy.start()
        sends.append(copy)
    own = zf[z]
    for d in steps:
        origin = lax.rem(z + 8 - d, 8)
        send(zs.at[0], zr.at[origin], zs_s.at[d - 1], zs_r.at[d - 1], {"pix_0": origin}).wait_recv()
        own = own + zr[origin].astype(F32)
    pieces[c, x, z] = own.astype(BF16)

    for d in steps:
        piece = pieces.at[c, x, z]
        peer = lax.rem(z + d, 8)
        copy = send(piece, piece, pz_s.at[d - 1], pz_r.at[d - 1], {"pix_0": peer})
        copy.start()
        sends.append(copy)
    for d in (0,) + steps:
        origin = lax.rem(z + 8 - d, 8)
        piece = pieces.at[c, x, origin]
        if d:
            send(piece, piece, pz_s.at[d - 1], pz_r.at[d - 1], {"pix_0": origin}).wait_recv()
        for e in (1, 3, 2):
            at = d * 3 + e - 1
            copy = send(piece, piece, px_s.at[at], px_r.at[at], {"obs": lax.rem(x + e, 4)})
            copy.start()
            sends.append(copy)
    for e in (0, 1, 3, 2):
        column = lax.rem(x + 4 - e, 4)
        if e:
            for d in (0,) + steps:
                at = d * 3 + e - 1
                piece = pieces.at[c, column, lax.rem(z + 8 - d, 8)]
                send(piece, piece, px_s.at[at], px_r.at[at], {"obs": column}).wait_recv()
        group = pieces.at[c, column]
        copy = send(group, group, pc_s.at[e], pc_r.at[e], {"pix_1": o})
        copy.start()
        sends.append(copy)
    for e in range(4):
        group = pieces.at[o, lax.rem(x + 4 - e, 4)]
        send(group, group, pc_s.at[e], pc_r.at[e], {"pix_1": o}).wait_recv()
    for cc in range(2):
        for xx in range(4):
            for zz in range(8):
                row = xx * lines + zz * wide
                out[pl.ds(row, wide), pl.ds(cc * 128, 128)] = pieces[cc, xx, zz].astype(F32)
    return sends


def finish_kernel(spec_hbm, part, out, spec, shards, total, half_out, half_in, turned, xs, xr,
                  zf, zs, zr, pieces, load_sems, gs, gr, *sems):
    y = lax.axis_index("chan")
    rows = part.shape[0]
    spec_copies = []
    for step, d in enumerate((0, 3, 1, 2)):
        block = pl.ds(pl.multiple_of(lax.rem(y + d, 4) * rows, rows), rows)
        copy = pltpu.make_async_copy(spec_hbm.at[block], spec.at[block], load_sems.at[step])
        copy.start()
        spec_copies.append(copy)
    greet((("obs", 4), ("pix_0", 8), ("pix_1", 2), ("chan", 4)))
    sends = gather_multiply(part, spec, spec_copies, shards, total, gs, gr)
    sends += add_up(total, out, half_out, half_in, turned, xs, xr, zf, zs, zr, pieces, sems)
    for copy in sends:
        copy.wait_send()


def finish(spectra, part):
    rows, features = part.shape
    channels = spectra.shape[1]
    dma = pltpu.SemaphoreType.DMA
    return pl.pallas_call(
        finish_kernel,
        out_shape=jax.ShapeDtypeStruct((channels, features), F32),
        in_specs=[pl.BlockSpec(memory_space=pl.ANY), pl.BlockSpec(memory_space=pltpu.VMEM)],
        out_specs=pl.BlockSpec(memory_space=pltpu.VMEM),
        scratch_shapes=[
            pltpu.VMEM(spectra.shape, BF16),
            pltpu.VMEM((4, rows, features), BF16),
            pltpu.VMEM((features, channels), F32),
            pltpu.VMEM((features // 2, channels), BF16),
            pltpu.VMEM((features // 2, channels), BF16),
            pltpu.VMEM((channels, features // 2), F32),
            pltpu.VMEM((4, channels // 4, features // 2), BF16),
            pltpu.VMEM((4, channels // 4, features // 2), BF16),
            pltpu.VMEM((8, channels // 32, features // 2), F32),
            pltpu.VMEM((8, channels // 32, features // 2), BF16),
            pltpu.VMEM((8, channels // 32, features // 2), BF16),
            pltpu.VMEM((2, 4, 8, channels // 32, features // 2), BF16),
            dma((4,)),
            dma((6,)),
            dma((6,)),
            dma(()),
            dma(()),
            dma((3,)),
            dma((3,)),
            dma((7,)),
            dma((7,)),
            dma((7,)),
            dma((7,)),
            dma((24,)),
            dma((24,)),
            dma((4,)),
            dma((4,)),
        ],
        compiler_params=pltpu.CompilerParams(collective_id=0, has_side_effects=True),
        name="finish",
    )(spectra, part)


def shards(spectra, enc_weight, pix_tile, pix_local, foot_weight, cotangent, adjoint, mixing):
    tile_count = lax.axis_size(PIX)
    groups = lax.axis_size("chan")
    tile_rows = cotangent.shape[0]
    feature_count = cotangent.shape[1]
    padded = extended(cotangent, ((PIX, 0),), HALO)
    block_count = tile_rows // HALO
    stacked = padded.reshape(block_count + 2, HALO, feature_count)
    windows = jnp.concatenate(
        (stacked[:block_count], stacked[1 : block_count + 1], stacked[2 : block_count + 2]), axis=1
    )
    anchor = lax.axis_index(PIX) * tile_rows - HALO
    block_start = (jnp.arange(block_count, dtype=jnp.int32) * HALO)[:, None]
    columns = jnp.arange(3 * HALO, dtype=jnp.int32)[None, None, :]
    summed = cotangent.astype(jnp.float32)
    for neighbor in range(NEIGH):
        within = (adjoint[neighbor] - anchor).reshape(block_count, HALO) - block_start
        selector = (within[:, :, None] == columns).astype(jnp.bfloat16)
        picked = jnp.einsum("bij,bje->bie", selector, windows, preferred_element_type=jnp.float32)
        summed = summed + picked.reshape(tile_rows, feature_count) * mixing[neighbor]
    pixel_grad = summed.astype(jnp.bfloat16)
    all_rows = spectra.shape[0]
    quarter = all_rows // groups
    capacity_part = 2 * quarter // tile_count
    pre = summed_on_arrival(
        jnp.dot(spectra, enc_weight, preferred_element_type=jnp.float32).astype(jnp.bfloat16),
        "chan",
        0,
    )
    first_row = lax.axis_index("chan") * quarter
    tile_ids = lax.dynamic_slice_in_dim(pix_tile[:, 0], first_row, quarter, 0)
    local_ids = lax.dynamic_slice_in_dim(pix_local, first_row, quarter, 0)
    weights = lax.dynamic_slice_in_dim(foot_weight, first_row, quarter, 0)
    fetched = fetch_rows(pixel_grad, tile_ids, local_ids, capacity_part)
    grad_part = pre_gradient(pre, fetched, weights)
    return finish(spectra, grad_part)


def solution(mesh):
    finer = Mesh(
        mesh.devices.reshape(mesh.shape["obs"], 8, 2, mesh.shape["chan"]),
        ("obs", "pix_0", "pix_1", "chan"),
    )
    placed = (
        P(OBS_PIX, "chan"),
        P("chan", None),
        P(OBS_PIX, None),
        P(OBS_PIX),
        P(OBS_PIX),
        P(PIX, None),
        P(None, PIX),
        P(),
    )
    return jax.shard_map(
        shards, mesh=finer, in_specs=placed, out_specs=P("chan", None), check_vma=False
    )
```

```python
import jax
import jax.numpy as jnp
from jax import lax
from jax.experimental import pallas as pl
from jax.experimental.pallas import tpu as pltpu
from jax.sharding import Mesh
from jax.sharding import PartitionSpec as P

TILE = 4096
CAP = 64
STEPS = (4, 3, 5, 2, 6, 1, 7, 0)
PIX = ("pix_0", "pix_1")
OBS_PIX = ("obs", "pix_0", "pix_1")
AXES = ("obs", "pix_0", "pix_1", "chan")
BF16 = jnp.bfloat16
F32 = jnp.float32


def send(source, target, send_sem, recv_sem, where):
    return pltpu.make_async_remote_copy(
        src_ref=source,
        dst_ref=target,
        send_sem=send_sem,
        recv_sem=recv_sem,
        device_id=where,
        device_id_type=pl.DeviceIdType.MESH,
    )


def greet():
    barrier = pltpu.get_barrier_semaphore()
    x, z, c, y = (lax.axis_index(name) for name in AXES)
    peers = [{"obs": lax.rem(x + d, 4)} for d in range(1, 4)]
    peers += [{"chan": lax.rem(y + d, 4)} for d in range(1, 4)]
    for d in range(8):
        for e in range(2):
            if d or e:
                peers.append({"pix_0": lax.rem(z + d, 8), "pix_1": lax.rem(c + e, 2)})
    for peer in peers:
        pl.semaphore_signal(
            barrier, inc=1, device_id=peer, device_id_type=pl.DeviceIdType.MESH
        )
    return barrier, len(peers)


def gather_multiply(part, spec, shards, total, gs, gr):
    y = lax.axis_index("chan")
    right, left, far = lax.rem(y + 1, 4), lax.rem(y + 3, 4), lax.rem(y + 2, 4)
    rows = part.shape[0]
    lo, hi = pl.ds(0, rows // 2), pl.ds(rows // 2, rows // 2)
    to_right, to_left = {"chan": right}, {"chan": left}
    sends = [
        send(part.at[lo], shards.at[y, lo], gs.at[0], gr.at[0], to_right),
        send(part.at[hi], shards.at[y, hi], gs.at[1], gr.at[1], to_left),
        send(part.at[hi], shards.at[y, hi], gs.at[2], gr.at[2], to_right),
        send(part.at[lo], shards.at[y, lo], gs.at[3], gr.at[3], to_left),
    ]
    for copy in sends:
        copy.start()

    width = total.shape[1] // 3

    def multiply(gradient, owner, step):
        turned = jnp.transpose(gradient.astype(F32)).astype(BF16)
        for n in range(3):
            columns = pl.ds(n * width, width)
            block = spec[pl.ds(pl.multiple_of(owner * rows, rows), rows), columns]
            product = jnp.dot(turned, block, preferred_element_type=F32)
            if step:
                total[:, columns] += product
            else:
                total[:, columns] = product

    multiply(part[...], y, 0)
    send(part.at[lo], shards.at[left, lo], gs.at[0], gr.at[0], to_right).wait_recv()
    sends.append(send(shards.at[left, lo], shards.at[left, lo], gs.at[4], gr.at[4], to_right))
    sends[4].start()
    send(part.at[hi], shards.at[right, hi], gs.at[1], gr.at[1], to_left).wait_recv()
    sends.append(send(shards.at[right, hi], shards.at[right, hi], gs.at[5], gr.at[5], to_left))
    sends[5].start()
    send(part.at[hi], shards.at[left, hi], gs.at[2], gr.at[2], to_right).wait_recv()
    multiply(shards[left], left, 1)
    send(part.at[lo], shards.at[right, lo], gs.at[3], gr.at[3], to_left).wait_recv()
    multiply(shards[right], right, 2)
    send(part.at[lo], shards.at[far, lo], gs.at[4], gr.at[4], to_right).wait_recv()
    send(part.at[hi], shards.at[far, hi], gs.at[5], gr.at[5], to_left).wait_recv()
    multiply(shards[far], far, 3)
    return sends


def add_up(total, out, half_out, half_in, turned, xs, xr, zf, zs, zr, pieces, sems):
    core_s, core_r, xs_s, xs_r, zs_s, zs_r, pz_s, pz_r, px_s, px_r, pc_s, pc_r = sems
    x, z, c = (lax.axis_index(name) for name in ("obs", "pix_0", "pix_1"))
    o = 1 - c
    lines, wide = xs.shape[1], zf.shape[1]
    sends = []

    half_out[...] = total[pl.ds(pl.multiple_of(o * 128, 128), 128), :].astype(BF16)
    swap = send(half_out, half_in, core_s, core_r, {"pix_1": o})
    swap.start()
    sends.append(swap)
    swap.wait_recv()
    mine = pl.ds(pl.multiple_of(c * 128, 128), 128)
    for j in range(total.shape[1] // 128):
        block = pl.ds(j * 128, 128)
        turned[block, :] = jnp.transpose(total[mine, block] + half_in[:, block].astype(F32))

    for j in range(4):
        xs[j] = turned[pl.ds(j * lines, lines), :].astype(BF16)
    for d in (1, 3, 2):
        peer = lax.rem(x + d, 4)
        copy = send(xs.at[peer], xr.at[x], xs_s.at[d - 1], xs_r.at[d - 1], {"obs": peer})
        copy.start()
        sends.append(copy)
    summed = turned[pl.ds(pl.multiple_of(x * lines, 8), lines), :]
    for d in (1, 3, 2):
        origin = lax.rem(x + 4 - d, 4)
        send(xs.at[0], xr.at[origin], xs_s.at[d - 1], xs_r.at[d - 1], {"obs": origin}).wait_recv()
        summed = summed + xr[origin].astype(F32)
    turned[pl.ds(0, lines), :] = summed

    for j in range(8):
        zf[j] = turned[pl.ds(j * wide, wide), :]
        zs[j] = zf[j].astype(BF16)
    steps = (1, 7, 2, 6, 3, 5, 4)
    for d in steps:
        peer = lax.rem(z + d, 8)
        copy = send(zs.at[peer], zr.at[z], zs_s.at[d - 1], zs_r.at[d - 1], {"pix_0": peer})
        copy.start()
        sends.append(copy)
    own = zf[z]
    for d in steps:
        origin = lax.rem(z + 8 - d, 8)
        send(zs.at[0], zr.at[origin], zs_s.at[d - 1], zs_r.at[d - 1], {"pix_0": origin}).wait_recv()
        own = own + zr[origin].astype(F32)
    pieces[c, x, z] = own.astype(BF16)

    for d in steps:
        piece = pieces.at[c, x, z]
        peer = lax.rem(z + d, 8)
        copy = send(piece, piece, pz_s.at[d - 1], pz_r.at[d - 1], {"pix_0": peer})
        copy.start()
        sends.append(copy)
    for d in (0,) + steps:
        origin = lax.rem(z + 8 - d, 8)
        piece = pieces.at[c, x, origin]
        if d:
            send(piece, piece, pz_s.at[d - 1], pz_r.at[d - 1], {"pix_0": origin}).wait_recv()
        for e in (1, 3, 2):
            at = d * 3 + e - 1
            copy = send(piece, piece, px_s.at[at], px_r.at[at], {"obs": lax.rem(x + e, 4)})
            copy.start()
            sends.append(copy)
    for e in (0, 1, 3, 2):
        column = lax.rem(x + 4 - e, 4)
        if e:
            for d in (0,) + steps:
                at = d * 3 + e - 1
                piece = pieces.at[c, column, lax.rem(z + 8 - d, 8)]
                send(piece, piece, px_s.at[at], px_r.at[at], {"obs": column}).wait_recv()
        group = pieces.at[c, column]
        copy = send(group, group, pc_s.at[e], pc_r.at[e], {"pix_1": o})
        copy.start()
        sends.append(copy)
    for e in range(4):
        group = pieces.at[o, lax.rem(x + 4 - e, 4)]
        send(group, group, pc_s.at[e], pc_r.at[e], {"pix_1": o}).wait_recv()
    for cc in range(2):
        for xx in range(4):
            for zz in range(8):
                row = xx * lines + zz * wide
                out[pl.ds(row, wide), pl.ds(cc * 128, 128)] = pieces[cc, xx, zz].astype(F32)
    return sends


def one_hot(condition):
    return jnp.where(condition, 1.0, 0.0).astype(BF16)


def iota(shape, dim):
    return lax.broadcasted_iota(jnp.int32, shape, dim)


def own_rows(ref, y):
    return jnp.concatenate([ref[pl.ds(4 * y + j, 1), :] for j in range(4)], axis=1)


def ask(tile, local, weight, y, asked, columns):
    tiles, locals_, weights = own_rows(tile, y), own_rows(local, y), own_rows(weight, y)
    rows = tiles.shape[1]
    named = jnp.broadcast_to(tiles, (16, rows)) == iota((16, rows), 0)
    earlier = one_hot(iota((rows, rows), 0) < iota((rows, rows), 1))
    counts = jnp.dot(one_hot(named), earlier, preferred_element_type=F32)
    rank = jnp.sum(jnp.where(named, counts, 0.0), axis=0, keepdims=True)
    placed = one_hot(jnp.broadcast_to(rank, (128, rows)) == iota((128, rows), 0).astype(F32))
    high = lax.shift_right_logical(locals_, 6)
    low = locals_ - high * 64
    wanted = jnp.zeros((16, 128), F32)
    for digit, scale in ((high, 64.0), (low, 1.0)):
        held = jnp.where(named, jnp.broadcast_to(digit.astype(F32), (16, rows)), 0.0).astype(BF16)
        wanted += scale * lax.dot_general(
            held, placed, (((1,), (1,)), ((), ())), preferred_element_type=F32
        )
    for t in range(16):
        asked[t] = wanted[t : t + 1, :]
    slot = tiles.astype(F32) * CAP + rank
    both = jnp.where(iota((128, rows), 0) == 0, jnp.broadcast_to(slot, (128, rows)),
                     jnp.broadcast_to(weights, (128, rows)))
    for j in range(rows // 128):
        block = pl.ds(j * 128, 128)
        columns[block, :] = jnp.transpose(both[:, j * 128 : (j + 1) * 128])


def spread(cot, adjoint, mixing, table, tile):
    block = 128
    lanes = iota((block, 3 * block), 1).astype(F32)

    def body(b, carry):
        start = pl.multiple_of(b * block, block)
        first = tile * TILE + start - block
        within = (adjoint[:, pl.ds(start, block)] - first).astype(F32)
        within = jnp.transpose(within)
        window = cot[pl.ds(start, 3 * block), :]
        total = window[block : 2 * block].astype(F32)
        for k in range(8):
            chosen = one_hot(jnp.broadcast_to(within[:, k : k + 1], lanes.shape) == lanes)
            picked = jnp.dot(chosen, window, preferred_element_type=F32)
            total = total + picked * mixing[pl.ds(k, 1), :]
        table[pl.ds(start, block), :] = total.astype(BF16)
        return carry

    lax.fori_loop(0, TILE // block, body, 0, unroll=2)


def answer(requests, table, start, answers):
    step = 512
    wanted = jnp.concatenate(
        [requests[0:CAP, k : k + 1] for k in range(start, start + 8)], axis=0
    )
    wanted = jnp.broadcast_to(wanted, (8 * CAP, step))
    lanes = iota((8 * CAP, step), 1).astype(F32)
    total = jnp.zeros((8 * CAP, table.shape[1]), F32)
    for j in range(TILE // step):
        chosen = one_hot(wanted - float(j * step) == lanes)
        total += jnp.dot(chosen, table[pl.ds(j * step, step), :], preferred_element_type=F32)
    for k in range(8):
        answers[start + k] = total[k * CAP : (k + 1) * CAP].astype(BF16)


def sums_of_parts(spec, spec_copies, weight, parts, parts_in, rs, rr, before_sends):
    y = lax.axis_index("chan")
    rows = parts.shape[1]
    sends = []
    for step, d in enumerate((2, 1, 3, 0)):
        peer = lax.rem(y + d, 4)
        spec_copies[step].wait()
        block = spec[pl.ds(pl.multiple_of(peer * rows, rows), rows), :]
        parts[peer] = jnp.dot(block, weight[...], preferred_element_type=F32).astype(BF16)
        if step == 0:
            before_sends()
        if d:
            copy = send(parts.at[peer], parts_in.at[y], rs.at[d - 1], rr.at[d - 1], {"chan": peer})
            copy.start()
            sends.append(copy)
    return sends


def whole_kernel(spec_hbm, weight, tile, local, foot, cot_hbm, adjoint, mixing, out, spec, cot,
                 table, parts, parts_in, asked, asked_in, square, columns, answers, answers_in,
                 part, shards, total, half_out, half_in, turned, xs, xr, zf, zs, zr, pieces,
                 result, load_sems, cot_sem, halo_s, halo_r, ask_s, ask_r, ans_s, ans_r, rs, rr,
                 gs, gr, *sems):
    x, z, c, y = (lax.axis_index(name) for name in AXES)
    me = z * 2 + c
    rows = part.shape[0]
    barrier, count = greet()
    spec_copies = []
    for step, d in enumerate((2, 1, 3, 0)):
        block = pl.ds(pl.multiple_of(lax.rem(y + d, 4) * rows, rows), rows)
        copy = pltpu.make_async_copy(spec_hbm.at[block], spec.at[block], load_sems.at[step])
        copy.start()
        spec_copies.append(copy)
    cot_copy = pltpu.make_async_copy(cot_hbm, cot.at[pl.ds(128, TILE)], cot_sem)
    cot_copy.start()
    ask(tile, local, foot, y, asked, columns)
    sends = []

    after = {"pix_0": lax.rem(z + c, 8), "pix_1": 1 - c}
    before = {"pix_0": lax.rem(z + 7 + c, 8), "pix_1": 1 - c}
    halos = [
        send(cot_hbm.at[pl.ds(0, 128)], cot.at[pl.ds(TILE + 128, 128)], halo_s.at[0],
             halo_r.at[0], before),
        send(cot_hbm.at[pl.ds(TILE - 128, 128)], cot.at[pl.ds(0, 128)], halo_s.at[1],
             halo_r.at[1], after),
    ]
    order = [(d, e) for d in STEPS for e in (1, 0)]

    def pair(k, ahead):
        d, e = order[k]
        other = lax.rem(c + e, 2)
        return lax.rem(z + (d if ahead else 8 - d), 8), other

    def first_sends():
        pl.semaphore_wait(barrier, count)
        for k in range(15):
            zz, cc = pair(k, True)
            copy = send(asked.at[zz * 2 + cc], asked_in.at[me], ask_s.at[k], ask_r.at[k],
                        {"pix_0": zz, "pix_1": cc})
            copy.start()
            sends.append(copy)
        for copy in halos:
            copy.start()
            sends.append(copy)

    sends += sums_of_parts(spec, spec_copies, weight, parts, parts_in, rs, rr, first_sends)
    cot_copy.wait()
    for copy in halos:
        copy.wait_recv()
    spread(cot, adjoint, mixing, table, me)

    square[...] = jnp.zeros_like(square)
    for k in range(15):
        zz, cc = pair(k, False)
        send(asked.at[0], asked_in.at[zz * 2 + cc], ask_s.at[k], ask_r.at[k],
             {"pix_0": zz, "pix_1": cc}).wait_recv()
        square[pl.ds(k, 1), :] = asked_in[zz * 2 + cc]
    square[pl.ds(15, 1), :] = asked[me]
    requests = jnp.transpose(square[...])
    for start in (0, 8):
        answer(requests, table, start, answers)
        for k in range(start, min(start + 8, 15)):
            zz, cc = pair(k, False)
            copy = send(answers.at[k], answers_in.at[me], ans_s.at[k], ans_r.at[k],
                        {"pix_0": zz, "pix_1": cc})
            copy.start()
            sends.append(copy)
    answers_in[me] = answers[15]

    pre = jnp.zeros((rows, part.shape[1]), F32)
    for d in (1, 3, 2):
        origin = lax.rem(y + 4 - d, 4)
        send(parts.at[0], parts_in.at[origin], rs.at[d - 1], rr.at[d - 1],
             {"chan": origin}).wait_recv()
        pre = pre + parts_in[origin].astype(F32)
    pre = pre + parts[y].astype(F32)
    sigma = 1.0 / (1.0 + jnp.exp(-pre))
    result[pl.ds(0, rows), :] = columns[:, 1:2] * (sigma * (1.0 + pre * (1.0 - sigma)))
    slots = 16 * CAP
    chosen = one_hot(
        jnp.broadcast_to(columns[:, 0:1], (rows, slots)) == iota((rows, slots), 1).astype(F32)
    )
    for k in range(15):
        zz, cc = pair(k, True)
        send(answers.at[0], answers_in.at[zz * 2 + cc], ans_s.at[k], ans_r.at[k],
             {"pix_0": zz, "pix_1": cc}).wait_recv()
    rows_in = answers_in[...].reshape(slots, part.shape[1])
    fetched = jnp.dot(chosen, rows_in, preferred_element_type=F32)
    part[...] = (result[pl.ds(0, rows), :] * fetched).astype(BF16)

    sends += gather_multiply(part, spec, shards, total, gs, gr)
    sends += add_up(total, result, half_out, half_in, turned, xs, xr, zf, zs, zr, pieces, sems)
    out[...] = result[...].astype(out.dtype)
    for copy in sends:
        copy.wait_send()


def shards(spectra, enc_weight, pix_tile, pix_local, foot_weight, cotangent, adjoint, mixing):
    rows, features = spectra.shape[0] // 4, cotangent.shape[1]
    channels = spectra.shape[1]
    dma = pltpu.SemaphoreType.DMA
    vmem = pl.BlockSpec(memory_space=pltpu.VMEM)
    anywhere = pl.BlockSpec(memory_space=pl.ANY)
    half, line, wide = features // 2, channels // 4, channels // 32
    encoded = pl.pallas_call(
        whole_kernel,
        out_shape=jax.ShapeDtypeStruct((channels, features), BF16),
        in_specs=[anywhere, vmem, vmem, vmem, vmem, anywhere, vmem, vmem],
        out_specs=vmem,
        scratch_shapes=[
            pltpu.VMEM(spectra.shape, BF16),
            pltpu.VMEM((TILE + 256, features), BF16),
            pltpu.VMEM((TILE, features), BF16),
            pltpu.VMEM((4, rows, features), BF16),
            pltpu.VMEM((4, rows, features), BF16),
            pltpu.VMEM((16, 1, 128), F32),
            pltpu.VMEM((16, 1, 128), F32),
            pltpu.VMEM((128, 128), F32),
            pltpu.VMEM((rows, 128), F32),
            pltpu.VMEM((16, CAP, features), BF16),
            pltpu.VMEM((16, CAP, features), BF16),
            pltpu.VMEM((rows, features), BF16),
            pltpu.VMEM((4, rows, features), BF16),
            pltpu.VMEM((features, channels), F32),
            pltpu.VMEM((half, channels), BF16),
            pltpu.VMEM((half, channels), BF16),
            pltpu.VMEM((channels, half), F32),
            pltpu.VMEM((4, line, half), BF16),
            pltpu.VMEM((4, line, half), BF16),
            pltpu.VMEM((8, wide, half), F32),
            pltpu.VMEM((8, wide, half), BF16),
            pltpu.VMEM((8, wide, half), BF16),
            pltpu.VMEM((2, 4, 8, wide, half), BF16),
            pltpu.VMEM((channels, features), F32),
        ]
        + [
            dma(shape)
            for shape in [(4,), ()]
            + [(n,) for n in (2, 2, 15, 15, 15, 15, 3, 3, 6, 6)]
            + [(), ()]
            + [(n,) for n in (3, 3, 7, 7, 7, 7, 24, 24, 4, 4)]
        ],
        compiler_params=pltpu.CompilerParams(collective_id=0, has_side_effects=True),
        name="whole",
    )(
        spectra,
        enc_weight,
        pix_tile.reshape(16, 128),
        pix_local.reshape(16, 128),
        foot_weight.reshape(16, 128),
        cotangent,
        adjoint,
        mixing,
    )
    return encoded.astype(F32)


def solution(mesh):
    finer = Mesh(
        mesh.devices.reshape(mesh.shape["obs"], 8, 2, mesh.shape["chan"]),
        ("obs", "pix_0", "pix_1", "chan"),
    )
    placed = (
        P(OBS_PIX, "chan"),
        P("chan", None),
        P(OBS_PIX, None),
        P(OBS_PIX),
        P(OBS_PIX),
        P(PIX, None),
        P(None, PIX),
        P(),
    )
    return jax.shard_map(
        shards, mesh=finer, in_specs=placed, out_specs=P("chan", None), check_vma=False
    )
```

```python
import jax
import jax.numpy as jnp
from jax import lax
from jax.experimental import pallas as pl
from jax.experimental.pallas import tpu as pltpu
from jax.sharding import Mesh
from jax.sharding import PartitionSpec as P

TILE = 4096
CAP = 64
SIDE = 128
STEPS = (4, 3, 5, 2, 6, 1, 7, 0)
PIX = ("pix_0", "pix_1")
OBS_PIX = ("obs", "pix_0", "pix_1")
AXES = ("obs", "pix_0", "pix_1", "chan")
BF16 = jnp.bfloat16
F32 = jnp.float32


def send(source, target, send_sem, recv_sem, where):
    return pltpu.make_async_remote_copy(
        src_ref=source,
        dst_ref=target,
        send_sem=send_sem,
        recv_sem=recv_sem,
        device_id=where,
        device_id_type=pl.DeviceIdType.MESH,
    )


def greet():
    barrier = pltpu.get_barrier_semaphore()
    x, z, c, y = (lax.axis_index(name) for name in AXES)
    peers = [{"obs": lax.rem(x + d, 4)} for d in range(1, 4)]
    peers += [{"chan": lax.rem(y + d, 4)} for d in range(1, 4)]
    for d in range(8):
        for e in range(2):
            if d or e:
                peers.append({"pix_0": lax.rem(z + d, 8), "pix_1": lax.rem(c + e, 2)})
    for peer in peers:
        pl.semaphore_signal(
            barrier, inc=1, device_id=peer, device_id_type=pl.DeviceIdType.MESH
        )
    return barrier, len(peers)


def one_hot(condition):
    return jnp.where(condition, 1.0, 0.0).astype(BF16)


def iota(shape, dim):
    return lax.broadcasted_iota(jnp.int32, shape, dim)


def own_rows(ref, y):
    return jnp.concatenate([ref[pl.ds(4 * y + j, 1), :] for j in range(4)], axis=1)


def ask(tile, local, weight, y, asked, columns):
    tiles, locals_, weights = own_rows(tile, y), own_rows(local, y), own_rows(weight, y)
    rows = tiles.shape[1]
    named = jnp.broadcast_to(tiles, (16, rows)) == iota((16, rows), 0)
    earlier = one_hot(iota((rows, rows), 0) < iota((rows, rows), 1))
    counts = jnp.dot(one_hot(named), earlier, preferred_element_type=F32)
    rank = jnp.sum(jnp.where(named, counts, 0.0), axis=0, keepdims=True)
    placed = one_hot(jnp.broadcast_to(rank, (128, rows)) == iota((128, rows), 0).astype(F32))
    high = lax.shift_right_logical(locals_, 6)
    low = locals_ - high * 64
    wanted = jnp.zeros((16, 128), F32)
    for digit, scale in ((high, 64.0), (low, 1.0)):
        held = jnp.where(named, jnp.broadcast_to(digit.astype(F32), (16, rows)), 0.0).astype(BF16)
        wanted += scale * lax.dot_general(
            held, placed, (((1,), (1,)), ((), ())), preferred_element_type=F32
        )
    for t in range(16):
        asked[t] = wanted[t : t + 1, :]
    slot = tiles.astype(F32) * CAP + rank
    both = jnp.where(iota((128, rows), 0) == 0, jnp.broadcast_to(slot, (128, rows)),
                     jnp.broadcast_to(weights, (128, rows)))
    for j in range(rows // 128):
        block = pl.ds(j * 128, 128)
        columns[block, :] = jnp.transpose(both[:, j * 128 : (j + 1) * 128])


def pixel_block(b, cot, adjoint, mixing, table, tile):
    block = SIDE
    lanes = iota((block, 3 * block), 1).astype(F32)
    start = pl.multiple_of(b * block, block)
    first = tile * TILE + start - block
    within = jnp.transpose((adjoint[:, pl.ds(start, block)] - first).astype(F32))
    window = cot[pl.ds(start, 3 * block), :]
    wide = (block, window.shape[1])
    ahead = jnp.broadcast_to(within[:, 0:1], wide) - iota(wide, 0).astype(F32) > 128.0
    edge = jnp.where(ahead, window[2 * block :].astype(F32), window[:block].astype(F32))
    total = window[block : 2 * block].astype(F32) + edge * mixing[pl.ds(0, 1), :]
    for k in range(1, 8):
        chosen = one_hot(jnp.broadcast_to(within[:, k : k + 1], lanes.shape) == lanes)
        picked = jnp.dot(chosen, window, preferred_element_type=F32)
        total = total + picked * mixing[pl.ds(k, 1), :]
    table[pl.ds(start, block), :] = total.astype(BF16)


def answer(requests, table, start, answers):
    step = 512
    wanted = jnp.concatenate(
        [requests[0:CAP, k : k + 1] for k in range(start, start + 8)], axis=0
    )
    wanted = jnp.broadcast_to(wanted, (8 * CAP, step))
    lanes = iota((8 * CAP, step), 1).astype(F32)
    total = jnp.zeros((8 * CAP, table.shape[1]), F32)
    for j in range(TILE // step):
        chosen = one_hot(wanted - float(j * step) == lanes)
        total += jnp.dot(chosen, table[pl.ds(j * step, step), :], preferred_element_type=F32)
    for k in range(8):
        for h in range(2):
            rows = total[k * CAP : (k + 1) * CAP, h * SIDE : (h + 1) * SIDE]
            answers[h, start + k] = rows.astype(BF16)


def whole_kernel(spec_hbm, weight, tile, local, foot, cot_hbm, adjoint, mixing, out, spec, cot,
                 table, parts, parts_in, relay, asked, asked_in, square, columns, answers,
                 answers_in, slope, chosen, part, shards, total, turned, cs, cr, mine, xs, xr,
                 xsum, zf, zs, zr, pieces, result, load_sems, cot_sem, halo_s, halo_r, ask_s,
                 ask_r, ans_s, ans_r, rs, rr, gs, gr, core_s, core_r, xs_s, xs_r, zs_s, zs_r,
                 pz_s, pz_r, px_s, px_r, pc_s, pc_r):
    x, z, c, y = (lax.axis_index(name) for name in AXES)
    o = 1 - c
    me = z * 2 + c
    rows = part.shape[1]
    right, left, far = lax.rem(y + 1, 4), lax.rem(y + 3, 4), lax.rem(y + 2, 4)
    to_right, to_left = {"chan": right}, {"chan": left}
    lo, hi = pl.ds(0, rows // 2), pl.ds(rows // 2, rows // 2)
    near = (1, 3, 2)
    ring = (1, 7, 2, 6, 3, 5, 4)
    sends = []

    def go(*args):
        copy = send(*args)
        copy.start()
        sends.append(copy)

    def arrived(*args):
        send(*args).wait_recv()

    barrier, count = greet()
    cot_copy = pltpu.make_async_copy(cot_hbm, cot.at[pl.ds(128, TILE)], cot_sem)
    cot_copy.start()
    owners = (far, right, left, y)
    spec_copies = []
    for step, owner in enumerate(owners):
        block = pl.ds(pl.multiple_of(owner * rows, rows), rows)
        copy = pltpu.make_async_copy(spec_hbm.at[block], spec.at[block], load_sems.at[step])
        copy.start()
        spec_copies.append(copy)
    ask(tile, local, foot, y, asked, columns)
    cot_copy.wait()

    order = [(d, e) for d in STEPS for e in (1, 0)]

    def pair(k, ahead):
        d, e = order[k]
        return lax.rem(z + (d if ahead else 8 - d), 8), lax.rem(c + e, 2)

    def pixels(step):
        owner = owners[step]

        def group(i, carry):
            for j in range(4):
                b = lax.rem(8 * step + 4 * i + j + 1, TILE // SIDE)
                pixel_block(b, cot, adjoint, mixing, table, me)
            half = pl.multiple_of(i * (rows // 2), rows // 2)
            block = spec[pl.ds(pl.multiple_of(owner * rows + half, rows // 2), rows // 2), :]
            product = jnp.dot(block, weight[...], preferred_element_type=F32)
            parts[owner, pl.ds(half, rows // 2), :] = product.astype(BF16)
            return carry

        spec_copies[step].wait()
        lax.fori_loop(0, 2, group, 0)

    after = {"pix_0": lax.rem(z + c, 8), "pix_1": o}
    before = {"pix_0": lax.rem(z + 7 + c, 8), "pix_1": o}
    pixels(0)
    pl.semaphore_wait(barrier, count)
    for k in range(15):
        zz, cc = pair(k, True)
        go(asked.at[zz * 2 + cc], asked_in.at[me], ask_s.at[k], ask_r.at[k],
           {"pix_0": zz, "pix_1": cc})
    ends = cot.at[pl.ds(0, 128)], cot.at[pl.ds(TILE + 128, 128)]
    go(cot_hbm.at[pl.ds(0, 128)], ends[1], halo_s.at[0], halo_r.at[0], before)
    go(cot_hbm.at[pl.ds(TILE - 128, 128)], ends[0], halo_s.at[1], halo_r.at[1], after)
    go(parts.at[far, lo], relay.at[0], rs.at[0], rr.at[0], to_right)
    go(parts.at[far, hi], relay.at[1], rs.at[1], rr.at[1], to_left)
    pixels(1)
    go(parts.at[right], parts_in.at[y], rs.at[2], rr.at[2], to_right)
    pixels(2)
    go(parts.at[left], parts_in.at[y], rs.at[3], rr.at[3], to_left)
    arrived(parts.at[far, lo], relay.at[0], rs.at[0], rr.at[0], to_left)
    go(relay.at[0], parts_in.at[left, lo], rs.at[4], rr.at[4], to_right)
    arrived(parts.at[far, hi], relay.at[1], rs.at[1], rr.at[1], to_right)
    go(relay.at[1], parts_in.at[right, hi], rs.at[5], rr.at[5], to_left)
    arrived(cot_hbm.at[pl.ds(0, 128)], ends[1], halo_s.at[0], halo_r.at[0], after)
    arrived(cot_hbm.at[pl.ds(0, 128)], ends[0], halo_s.at[1], halo_r.at[1], before)
    pixels(3)

    square[...] = jnp.zeros_like(square)
    for k in range(15):
        zz, cc = pair(k, False)
        arrived(asked.at[0], asked_in.at[zz * 2 + cc], ask_s.at[k], ask_r.at[k],
                {"pix_0": zz, "pix_1": cc})
        square[pl.ds(k, 1), :] = asked_in[zz * 2 + cc]
    square[pl.ds(15, 1), :] = asked[me]
    requests = jnp.transpose(square[...])

    def reply(h, first, last):
        for k in range(first, last):
            zz, cc = pair(k, False)
            go(answers.at[h, k], answers_in.at[h, me], ans_s.at[h * 15 + k],
               ans_r.at[h * 15 + k], {"pix_0": zz, "pix_1": cc})

    answer(requests, table, 0, answers)
    reply(0, 0, 8)
    answer(requests, table, 8, answers)
    reply(0, 8, 15)
    reply(1, 0, 15)
    for h in range(2):
        answers_in[h, me] = answers[h, 15]

    slots = 16 * CAP
    chosen[...] = one_hot(
        jnp.broadcast_to(columns[:, 0:1], (rows, slots)) == iota((rows, slots), 1).astype(F32)
    )
    arrived(parts.at[0], parts_in.at[left], rs.at[2], rr.at[2], to_left)
    arrived(parts.at[0], parts_in.at[right], rs.at[3], rr.at[3], to_right)
    arrived(relay.at[0], parts_in.at[far, lo], rs.at[4], rr.at[4], to_left)
    arrived(relay.at[1], parts_in.at[far, hi], rs.at[5], rr.at[5], to_right)
    pre = parts[y].astype(F32)
    for origin in (left, right, far):
        pre = pre + parts_in[origin].astype(F32)
    sigma = 1.0 / (1.0 + jnp.exp(-pre))
    slope[...] = columns[:, 1:2] * (sigma * (1.0 + pre * (1.0 - sigma)))

    def fetch(h):
        for k in range(15):
            zz, cc = pair(k, True)
            arrived(answers.at[h, k], answers_in.at[h, zz * 2 + cc], ans_s.at[h * 15 + k],
                    ans_r.at[h * 15 + k], {"pix_0": zz, "pix_1": cc})
        rows_in = answers_in[h].reshape(slots, SIDE)
        fetched = jnp.dot(chosen[...], rows_in, preferred_element_type=F32)
        part[h] = (slope[:, h * SIDE : (h + 1) * SIDE] * fetched).astype(BF16)

    def multiply(h, gradient, owner, fresh=False):
        flat = jnp.transpose(gradient.astype(F32)).astype(BF16)
        width = spec.shape[1] // 3
        for n in range(3):
            cols = pl.ds(n * width, width)
            block = spec[pl.ds(pl.multiple_of(owner * rows, rows), rows), cols]
            product = jnp.dot(flat, block, preferred_element_type=F32)
            if fresh:
                total[h, :, cols] = product
            else:
                total[h, :, cols] += product

    def gather_start(h):
        i = h * 6
        mine_, store = part.at[h], shards.at[h]
        go(mine_.at[lo], store.at[y, lo], gs.at[i], gr.at[i], to_right)
        go(mine_.at[hi], store.at[y, hi], gs.at[i + 1], gr.at[i + 1], to_left)
        go(mine_.at[hi], store.at[y, hi], gs.at[i + 2], gr.at[i + 2], to_right)
        go(mine_.at[lo], store.at[y, lo], gs.at[i + 3], gr.at[i + 3], to_left)
        multiply(h, part[h], y, True)

    def gather_near(h):
        i = h * 6
        mine_, store = part.at[h], shards.at[h]
        arrived(mine_.at[lo], store.at[left, lo], gs.at[i], gr.at[i], to_left)
        go(store.at[left, lo], store.at[left, lo], gs.at[i + 4], gr.at[i + 4], to_right)
        arrived(mine_.at[hi], store.at[right, hi], gs.at[i + 1], gr.at[i + 1], to_right)
        go(store.at[right, hi], store.at[right, hi], gs.at[i + 5], gr.at[i + 5], to_left)
        arrived(mine_.at[hi], store.at[left, hi], gs.at[i + 2], gr.at[i + 2], to_left)
        multiply(h, shards[h, left], left)
        arrived(mine_.at[lo], store.at[right, lo], gs.at[i + 3], gr.at[i + 3], to_right)
        multiply(h, shards[h, right], right)

    core_lines, line, wide = mine.shape[1], xs.shape[2], zs.shape[2]

    def gather_far(h):
        i = h * 6
        store = shards.at[h]
        arrived(store.at[far, lo], store.at[far, lo], gs.at[i + 4], gr.at[i + 4], to_left)
        arrived(store.at[far, hi], store.at[far, hi], gs.at[i + 5], gr.at[i + 5], to_right)
        multiply(h, shards[h, far], far)
        for j in range(total.shape[2] // SIDE):
            block = pl.ds(j * SIDE, SIDE)
            turned[h, block, :] = jnp.transpose(total[h, :, block])
        theirs = pl.ds(pl.multiple_of(o * core_lines, 8), core_lines)
        cs[h] = turned[h, theirs, :].astype(BF16)
        go(cs.at[h], cr.at[h], core_s.at[h], core_r.at[h], {"pix_1": o})

    def core_sum(h):
        arrived(cs.at[h], cr.at[h], core_s.at[h], core_r.at[h], {"pix_1": o})
        ours = pl.ds(pl.multiple_of(c * core_lines, 8), core_lines)
        mine[h] = turned[h, ours, :] + cr[h].astype(F32)
        for j in range(4):
            xs[h, j] = mine[h, pl.ds(j * line, line), :].astype(BF16)
        for d in near:
            peer = lax.rem(x + d, 4)
            at = h * 3 + d - 1
            go(xs.at[h, peer], xr.at[h, x], xs_s.at[at], xs_r.at[at], {"obs": peer})

    def x_sum(h):
        summed = mine[h, pl.ds(pl.multiple_of(x * line, 8), line), :]
        for d in near:
            origin = lax.rem(x + 4 - d, 4)
            at = h * 3 + d - 1
            arrived(xs.at[h, 0], xr.at[h, origin], xs_s.at[at], xs_r.at[at], {"obs": origin})
            summed = summed + xr[h, origin].astype(F32)
        xsum[h] = summed
        for j in range(8):
            zf[h, j] = xsum[h, pl.ds(j * wide, wide), :]
            zs[h, j] = zf[h, j].astype(BF16)
        for d in ring:
            peer = lax.rem(z + d, 8)
            at = h * 7 + d - 1
            go(zs.at[h, peer], zr.at[h, z], zs_s.at[at], zs_r.at[at], {"pix_0": peer})

    def z_sum(h):
        own = zf[h, z]
        for d in ring:
            origin = lax.rem(z + 8 - d, 8)
            at = h * 7 + d - 1
            arrived(zs.at[h, 0], zr.at[h, origin], zs_s.at[at], zs_r.at[at], {"pix_0": origin})
            own = own + zr[h, origin].astype(F32)
        pieces[h, c, x, z] = own.astype(BF16)
        piece = pieces.at[h, c, x, z]
        for d in ring:
            at = h * 7 + d - 1
            go(piece, piece, pz_s.at[at], pz_r.at[at], {"pix_0": lax.rem(z + d, 8)})

    def z_gather(h):
        for d in (0,) + ring:
            origin = lax.rem(z + 8 - d, 8)
            piece = pieces.at[h, c, x, origin]
            if d:
                at = h * 7 + d - 1
                arrived(piece, piece, pz_s.at[at], pz_r.at[at], {"pix_0": origin})
            for e in near:
                at = (h * 8 + d) * 3 + e - 1
                go(piece, piece, px_s.at[at], px_r.at[at], {"obs": lax.rem(x + e, 4)})
        group = pieces.at[h, c, x]
        go(group, group, pc_s.at[h * 4], pc_r.at[h * 4], {"pix_1": o})

    def x_gather(h):
        for e in near:
            column = lax.rem(x + 4 - e, 4)
            for d in (0,) + ring:
                at = (h * 8 + d) * 3 + e - 1
                piece = pieces.at[h, c, column, lax.rem(z + 8 - d, 8)]
                arrived(piece, piece, px_s.at[at], px_r.at[at], {"obs": column})
            group = pieces.at[h, c, column]
            go(group, group, pc_s.at[h * 4 + e], pc_r.at[h * 4 + e], {"pix_1": o})

    def core_gather(h):
        for e in (0,) + near:
            group = pieces.at[h, o, lax.rem(x + 4 - e, 4)]
            arrived(group, group, pc_s.at[h * 4 + e], pc_r.at[h * 4 + e], {"pix_1": o})
        for cc in range(2):
            for xx in range(4):
                for zz in range(8):
                    row = cc * core_lines + xx * line + zz * wide
                    result[pl.ds(row, wide), :] = pieces[h, cc, xx, zz].astype(F32)
        out[:, h * SIDE : (h + 1) * SIDE] = result[...].astype(out.dtype)

    fetch(0)
    gather_start(0)
    gather_near(0)
    fetch(1)
    gather_start(1)
    gather_far(0)
    gather_near(1)
    core_sum(0)
    gather_far(1)
    x_sum(0)
    core_sum(1)
    z_sum(0)
    x_sum(1)
    z_gather(0)
    z_sum(1)
    x_gather(0)
    z_gather(1)
    core_gather(0)
    x_gather(1)
    core_gather(1)
    for copy in sends:
        copy.wait_send()


def shards(spectra, enc_weight, pix_tile, pix_local, foot_weight, cotangent, adjoint, mixing):
    rows, features = spectra.shape[0] // 4, cotangent.shape[1]
    channels = spectra.shape[1]
    dma = pltpu.SemaphoreType.DMA
    vmem = pl.BlockSpec(memory_space=pltpu.VMEM)
    anywhere = pl.BlockSpec(memory_space=pl.ANY)
    core, line, wide = channels // 2, channels // 8, channels // 64
    shapes = [
        (spectra.shape, BF16),
        ((TILE + 256, features), BF16),
        ((TILE, features), BF16),
        ((4, rows, features), BF16),
        ((4, rows, features), BF16),
        ((2, rows // 2, features), BF16),
        ((16, 1, 128), F32),
        ((16, 1, 128), F32),
        ((128, 128), F32),
        ((rows, 128), F32),
        ((2, 16, CAP, SIDE), BF16),
        ((2, 16, CAP, SIDE), BF16),
        ((rows, features), F32),
        ((rows, 16 * CAP), BF16),
        ((2, rows, SIDE), BF16),
        ((2, 4, rows, SIDE), BF16),
        ((2, SIDE, channels), F32),
        ((2, channels, SIDE), F32),
        ((2, core, SIDE), BF16),
        ((2, core, SIDE), BF16),
        ((2, core, SIDE), F32),
        ((2, 4, line, SIDE), BF16),
        ((2, 4, line, SIDE), BF16),
        ((2, line, SIDE), F32),
        ((2, 8, wide, SIDE), F32),
        ((2, 8, wide, SIDE), BF16),
        ((2, 8, wide, SIDE), BF16),
        ((2, 2, 4, 8, wide, SIDE), BF16),
        ((channels, SIDE), F32),
    ]
    counts = [2, 15, 30, 6, 12, 2, 6, 14, 14, 48, 8]
    encoded = pl.pallas_call(
        whole_kernel,
        out_shape=jax.ShapeDtypeStruct((channels, features), BF16),
        in_specs=[anywhere, vmem, vmem, vmem, vmem, anywhere, vmem, vmem],
        out_specs=vmem,
        scratch_shapes=[pltpu.VMEM(shape, kind) for shape, kind in shapes]
        + [dma((4,)), dma(())]
        + [dma((n,)) for n in counts for _ in range(2)],
        compiler_params=pltpu.CompilerParams(collective_id=0, has_side_effects=True),
        name="whole",
    )(
        spectra,
        enc_weight,
        pix_tile.reshape(16, 128),
        pix_local.reshape(16, 128),
        foot_weight.reshape(16, 128),
        cotangent,
        adjoint,
        mixing,
    )
    return encoded.astype(F32)


def solution(mesh):
    finer = Mesh(
        mesh.devices.reshape(mesh.shape["obs"], 8, 2, mesh.shape["chan"]),
        ("obs", "pix_0", "pix_1", "chan"),
    )
    placed = (
        P(OBS_PIX, "chan"),
        P("chan", None),
        P(OBS_PIX, None),
        P(OBS_PIX),
        P(OBS_PIX),
        P(PIX, None),
        P(None, PIX),
        P(),
    )
    return jax.shard_map(
        shards, mesh=finer, in_specs=placed, out_specs=P("chan", None), check_vma=False
    )
```

```python
import jax
import jax.numpy as jnp
from jax import lax
from jax.experimental import pallas as pl
from jax.experimental.pallas import tpu as pltpu
from jax.sharding import Mesh
from jax.sharding import PartitionSpec as P

TILE = 4096
CAP = 64
SIDE = 128
STEPS = (4, 3, 5, 2, 6, 1, 7, 0)
PIX = ("pix_0", "pix_1")
OBS_PIX = ("obs", "pix_0", "pix_1")
AXES = ("obs", "pix_0", "pix_1", "chan")
BF16 = jnp.bfloat16
F32 = jnp.float32


def send(source, target, send_sem, recv_sem, where):
    return pltpu.make_async_remote_copy(
        src_ref=source,
        dst_ref=target,
        send_sem=send_sem,
        recv_sem=recv_sem,
        device_id=where,
        device_id_type=pl.DeviceIdType.MESH,
    )


def greet():
    barrier = pltpu.get_barrier_semaphore()
    x, z, c, y = (lax.axis_index(name) for name in AXES)
    peers = [{"obs": lax.rem(x + d, 4)} for d in range(1, 4)]
    peers += [{"chan": lax.rem(y + d, 4)} for d in range(1, 4)]
    for d in range(8):
        for e in range(2):
            if d or e:
                peers.append({"pix_0": lax.rem(z + d, 8), "pix_1": lax.rem(c + e, 2)})
    for peer in peers:
        pl.semaphore_signal(
            barrier, inc=1, device_id=peer, device_id_type=pl.DeviceIdType.MESH
        )
    return barrier, len(peers)


def one_hot(condition):
    return jnp.where(condition, 1.0, 0.0).astype(BF16)


def iota(shape, dim):
    return lax.broadcasted_iota(jnp.int32, shape, dim)


def own_rows(ref, y):
    return jnp.concatenate([ref[pl.ds(4 * y + j, 1), :] for j in range(4)], axis=1)


def ask(tile, local, weight, y, asked, columns):
    tiles, locals_, weights = own_rows(tile, y), own_rows(local, y), own_rows(weight, y)
    rows = tiles.shape[1]
    named = jnp.broadcast_to(tiles, (16, rows)) == iota((16, rows), 0)
    earlier = one_hot(iota((rows, rows), 0) < iota((rows, rows), 1))
    counts = jnp.dot(one_hot(named), earlier, preferred_element_type=F32)
    rank = jnp.sum(jnp.where(named, counts, 0.0), axis=0, keepdims=True)
    placed = one_hot(jnp.broadcast_to(rank, (128, rows)) == iota((128, rows), 0).astype(F32))
    high = lax.shift_right_logical(locals_, 6)
    low = locals_ - high * 64
    wanted = jnp.zeros((16, 128), F32)
    for digit, scale in ((high, 64.0), (low, 1.0)):
        held = jnp.where(named, jnp.broadcast_to(digit.astype(F32), (16, rows)), 0.0).astype(BF16)
        wanted += scale * lax.dot_general(
            held, placed, (((1,), (1,)), ((), ())), preferred_element_type=F32
        )
    for t in range(16):
        asked[t] = jnp.clip(wanted[t : t + 1, :].astype(jnp.int32), 0, TILE - 1)
    slot = tiles.astype(F32) * CAP + rank
    both = jnp.where(iota((128, rows), 0) == 0, jnp.broadcast_to(slot, (128, rows)),
                     jnp.broadcast_to(weights, (128, rows)))
    for j in range(rows // 128):
        block = pl.ds(j * 128, 128)
        columns[block, :] = jnp.transpose(both[:, j * 128 : (j + 1) * 128])


def widen(cot, rows_of, first, count):
    for h in range(2):
        half = cot[pl.ds(first, count), h * SIDE : (h + 1) * SIDE].astype(F32)
        rows_of[pl.ds(2 * first + h, count, stride=2), :] = half


def whole_kernel(spec_hbm, weight_hbm, tile_hbm, local_hbm, foot_hbm, cot_hbm, adjoint_hbm,
                 mixing_hbm, out, weight, tile, local, foot, adjoint, mixing, spec, cot, rows_of, mixed, near_rows, formed, parts, parts_in, relay, asked, asked_in,
                 wanted, chip_wanted, *rest):
    lists, rest = rest[:8], rest[8:]
    (columns, answers, answers_in, slope, chosen, part, shards, total, turned, cs, cr, mine, xs, xr,
                 xsum, zf, zs, zr, pieces, result, load_sems, cot_sem, list_sems, want_sem,
     chip_sem, in_sems,
     halo_s, halo_r, ask_s, ask_r, ans_s, ans_r, rs, rr, gs, gr, core_s, core_r, xs_s, xs_r, zs_s,
     zs_r, pz_s, pz_r, px_s, px_r, pc_s, pc_r) = rest
    x, z, c, y = (lax.axis_index(name) for name in AXES)
    o = 1 - c
    me = z * 2 + c
    rows = part.shape[1]
    right, left, far = lax.rem(y + 1, 4), lax.rem(y + 3, 4), lax.rem(y + 2, 4)
    to_right, to_left = {"chan": right}, {"chan": left}
    lo, hi = pl.ds(0, rows // 2), pl.ds(rows // 2, rows // 2)
    near = (1, 3, 2)
    ring = (1, 7, 2, 6, 3, 5, 4)
    sends = []

    def go(*args):
        copy = send(*args)
        copy.start()
        sends.append(copy)

    def arrived(*args):
        send(*args).wait_recv()

    barrier, count = greet()
    operands = ((adjoint_hbm, adjoint), (tile_hbm, tile), (local_hbm, local), (foot_hbm, foot),
                (mixing_hbm, mixing), (weight_hbm, weight))
    loads = [pltpu.make_async_copy(a, b, in_sems.at[i]) for i, (a, b) in enumerate(operands)]
    for copy in loads[:5]:
        copy.start()
    cot_copy = pltpu.make_async_copy(cot_hbm, cot.at[pl.ds(128, TILE)], cot_sem)
    cot_copy.start()
    loads[5].start()
    loads[0].wait()
    inside = jnp.clip(adjoint[...] - (me * TILE - SIDE), 0, TILE + 2 * SIDE - 1)
    near_rows[...] = inside * 2
    list_copies = []
    for k in range(8):
        copy = pltpu.make_async_copy(near_rows.at[pl.ds(k, 1)], lists[k], list_sems.at[k])
        copy.start()
        list_copies.append(copy)
    for copy in loads[1:5]:
        copy.wait()
    ask(tile, local, foot, y, asked, columns)
    asked_in[me] = asked[me]
    owners = (far, right, left, y)
    spec_copies = []
    for step, owner in enumerate(owners):
        block = pl.ds(pl.multiple_of(owner * rows, rows), rows)
        copy = pltpu.make_async_copy(spec_hbm.at[block], spec.at[block], load_sems.at[step])
        copy.start()
        spec_copies.append(copy)
    for k in range(8):
        for h in range(2):
            mixed[pl.ds(2 * k + h, 1), :] = mixing[pl.ds(k, 1), h * SIDE : (h + 1) * SIDE]

    order = [(d, e) for d in STEPS for e in (1, 0)]

    def pair(k, ahead):
        d, e = order[k]
        return lax.rem(z + (d if ahead else 8 - d), 8), lax.rem(c + e, 2)

    after = {"pix_0": lax.rem(z + c, 8), "pix_1": o}
    before = {"pix_0": lax.rem(z + 7 + c, 8), "pix_1": o}
    pl.semaphore_wait(barrier, count)
    for k in range(15):
        zz, cc = pair(k, True)
        go(asked.at[zz * 2 + cc], asked_in.at[me], ask_s.at[k], ask_r.at[k],
           {"pix_0": zz, "pix_1": cc})
    ends = cot.at[pl.ds(0, SIDE)], cot.at[pl.ds(TILE + SIDE, SIDE)]
    go(cot_hbm.at[pl.ds(0, SIDE)], ends[1], halo_s.at[0], halo_r.at[0], before)
    go(cot_hbm.at[pl.ds(TILE - SIDE, SIDE)], ends[0], halo_s.at[1], halo_r.at[1], after)

    cot_copy.wait()

    def widen_step(i, carry):
        widen(cot, rows_of, pl.multiple_of(SIDE + i * 256, SIDE), 256)
        return carry

    lax.fori_loop(0, TILE // 256, widen_step, 0)

    loads[5].wait()

    def encode(step):
        owner = owners[step]
        spec_copies[step].wait()
        block = spec[pl.ds(pl.multiple_of(owner * rows, rows), rows), :]
        parts[owner] = jnp.dot(block, weight[...], preferred_element_type=F32).astype(BF16)

    encode(0)
    go(parts.at[far, lo], relay.at[0], rs.at[0], rr.at[0], to_right)
    go(parts.at[far, hi], relay.at[1], rs.at[1], rr.at[1], to_left)
    encode(1)
    go(parts.at[right], parts_in.at[y], rs.at[2], rr.at[2], to_right)
    encode(2)
    go(parts.at[left], parts_in.at[y], rs.at[3], rr.at[3], to_left)
    arrived(cot_hbm.at[pl.ds(0, SIDE)], ends[1], halo_s.at[0], halo_r.at[0], after)
    arrived(cot_hbm.at[pl.ds(0, SIDE)], ends[0], halo_s.at[1], halo_r.at[1], before)
    widen(cot, rows_of, 0, SIDE)
    widen(cot, rows_of, TILE + SIDE, SIDE)
    for copy in list_copies:
        copy.wait()

    def requested(k):
        zz, cc = pair(k, False)
        arrived(asked.at[0], asked_in.at[zz * 2 + cc], ask_s.at[k], ask_r.at[k],
                {"pix_0": zz, "pix_1": cc})

    def serve(k, source):
        zz, cc = pair(k, False)
        asker = zz * 2 + cc
        mix = [mixed[pl.ds(2 * n, 2), :] for n in range(8)]
        unroll = 16

        def some(i, carry):
            for u in range(unroll):
                at = i * unroll + u
                pixel = source[asker if source is wanted else cc, 0, at]
                row = rows_of[pl.ds(pixel * 2 + 2 * SIDE, 2), :]
                for n in range(8):
                    row = row + rows_of[pl.ds(lists[n][0, pixel], 2), :] * mix[n]
                formed[pl.ds(k % 2 * 2 * CAP + 2 * at, 2), :] = row
            return carry

        lax.fori_loop(0, CAP // unroll, some, 0)
        for h in range(2):
            half = formed[pl.ds(k % 2 * 2 * CAP + h, CAP, stride=2), :]
            answers[h, k] = half.astype(BF16)

    def reply(h, k):
        zz, cc = pair(k, False)
        go(answers.at[h, k], answers_in.at[h, me], ans_s.at[h * 15 + k], ans_r.at[h * 15 + k],
           {"pix_0": zz, "pix_1": cc})

    requested(14)
    chip_copy = pltpu.make_async_copy(asked_in.at[pl.ds(2 * z, 2)], chip_wanted, chip_sem)
    chip_copy.start()
    chip_copy.wait()
    serve(15, chip_wanted)
    serve(14, chip_wanted)
    reply(0, 14)
    for h in range(2):
        answers_in[h, me] = answers[h, 15]
    for k in range(14):
        requested(k)
    want_copy = pltpu.make_async_copy(asked_in, wanted, want_sem)
    want_copy.start()
    want_copy.wait()
    lag = 10
    for k in range(14):
        serve(k, wanted)
        reply(0, k)
        if k == 0:
            reply(1, 14)
        if k >= lag:
            reply(1, k - lag)
        if k == 3:
            arrived(parts.at[far, lo], relay.at[0], rs.at[0], rr.at[0], to_left)
            go(relay.at[0], parts_in.at[left, lo], rs.at[4], rr.at[4], to_right)
            arrived(parts.at[far, hi], relay.at[1], rs.at[1], rr.at[1], to_right)
            go(relay.at[1], parts_in.at[right, hi], rs.at[5], rr.at[5], to_left)
    for k in range(14 - lag, 14):
        reply(1, k)
    encode(3)

    slots = 16 * CAP
    chosen[...] = one_hot(
        jnp.broadcast_to(columns[:, 0:1], (rows, slots)) == iota((rows, slots), 1).astype(F32)
    )
    arrived(parts.at[0], parts_in.at[left], rs.at[2], rr.at[2], to_left)
    arrived(parts.at[0], parts_in.at[right], rs.at[3], rr.at[3], to_right)
    arrived(relay.at[0], parts_in.at[far, lo], rs.at[4], rr.at[4], to_left)
    arrived(relay.at[1], parts_in.at[far, hi], rs.at[5], rr.at[5], to_right)
    pre = parts[y].astype(F32)
    for origin in (left, right, far):
        pre = pre + parts_in[origin].astype(F32)
    sigma = 1.0 / (1.0 + jnp.exp(-pre))
    slope[...] = columns[:, 1:2] * (sigma * (1.0 + pre * (1.0 - sigma)))

    def fetch(h):
        for k in range(15):
            zz, cc = pair(k, True)
            arrived(answers.at[h, k], answers_in.at[h, zz * 2 + cc], ans_s.at[h * 15 + k],
                    ans_r.at[h * 15 + k], {"pix_0": zz, "pix_1": cc})
        rows_in = answers_in[h].reshape(slots, SIDE)
        fetched = jnp.dot(chosen[...], rows_in, preferred_element_type=F32)
        part[h] = (slope[:, h * SIDE : (h + 1) * SIDE] * fetched).astype(BF16)

    def multiply(h, gradient, owner, fresh=False):
        flat = jnp.transpose(gradient.astype(F32)).astype(BF16)
        width = spec.shape[1] // 3
        for n in range(3):
            cols = pl.ds(n * width, width)
            block = spec[pl.ds(pl.multiple_of(owner * rows, rows), rows), cols]
            product = jnp.dot(flat, block, preferred_element_type=F32)
            if fresh:
                total[h, :, cols] = product
            else:
                total[h, :, cols] += product

    def gather_start(h):
        i = h * 6
        mine_, store = part.at[h], shards.at[h]
        go(mine_.at[lo], store.at[y, lo], gs.at[i], gr.at[i], to_right)
        go(mine_.at[hi], store.at[y, hi], gs.at[i + 1], gr.at[i + 1], to_left)
        go(mine_.at[hi], store.at[y, hi], gs.at[i + 2], gr.at[i + 2], to_right)
        go(mine_.at[lo], store.at[y, lo], gs.at[i + 3], gr.at[i + 3], to_left)
        multiply(h, part[h], y, True)

    def gather_near(h):
        i = h * 6
        mine_, store = part.at[h], shards.at[h]
        arrived(mine_.at[lo], store.at[left, lo], gs.at[i], gr.at[i], to_left)
        go(store.at[left, lo], store.at[left, lo], gs.at[i + 4], gr.at[i + 4], to_right)
        arrived(mine_.at[hi], store.at[right, hi], gs.at[i + 1], gr.at[i + 1], to_right)
        go(store.at[right, hi], store.at[right, hi], gs.at[i + 5], gr.at[i + 5], to_left)
        arrived(mine_.at[hi], store.at[left, hi], gs.at[i + 2], gr.at[i + 2], to_left)
        multiply(h, shards[h, left], left)
        arrived(mine_.at[lo], store.at[right, lo], gs.at[i + 3], gr.at[i + 3], to_right)
        multiply(h, shards[h, right], right)

    core_lines, line, wide = mine.shape[1], xs.shape[2], zs.shape[2]

    def gather_far(h):
        i = h * 6
        store = shards.at[h]
        arrived(store.at[far, lo], store.at[far, lo], gs.at[i + 4], gr.at[i + 4], to_left)
        arrived(store.at[far, hi], store.at[far, hi], gs.at[i + 5], gr.at[i + 5], to_right)
        multiply(h, shards[h, far], far)
        for j in range(total.shape[2] // SIDE):
            block = pl.ds(j * SIDE, SIDE)
            turned[h, block, :] = jnp.transpose(total[h, :, block])
        theirs = pl.ds(pl.multiple_of(o * core_lines, 8), core_lines)
        cs[h] = turned[h, theirs, :].astype(BF16)
        go(cs.at[h], cr.at[h], core_s.at[h], core_r.at[h], {"pix_1": o})

    def core_sum(h):
        arrived(cs.at[h], cr.at[h], core_s.at[h], core_r.at[h], {"pix_1": o})
        ours = pl.ds(pl.multiple_of(c * core_lines, 8), core_lines)
        mine[h] = turned[h, ours, :] + cr[h].astype(F32)
        for j in range(4):
            xs[h, j] = mine[h, pl.ds(j * line, line), :].astype(BF16)
        for d in near:
            peer = lax.rem(x + d, 4)
            at = h * 3 + d - 1
            go(xs.at[h, peer], xr.at[h, x], xs_s.at[at], xs_r.at[at], {"obs": peer})

    def x_sum(h):
        summed = mine[h, pl.ds(pl.multiple_of(x * line, 8), line), :]
        for d in near:
            origin = lax.rem(x + 4 - d, 4)
            at = h * 3 + d - 1
            arrived(xs.at[h, 0], xr.at[h, origin], xs_s.at[at], xs_r.at[at], {"obs": origin})
            summed = summed + xr[h, origin].astype(F32)
        xsum[h] = summed
        for j in range(8):
            zf[h, j] = xsum[h, pl.ds(j * wide, wide), :]
            zs[h, j] = zf[h, j].astype(BF16)
        for d in ring:
            peer = lax.rem(z + d, 8)
            at = h * 7 + d - 1
            go(zs.at[h, peer], zr.at[h, z], zs_s.at[at], zs_r.at[at], {"pix_0": peer})

    def z_sum(h):
        own = zf[h, z]
        for d in ring:
            origin = lax.rem(z + 8 - d, 8)
            at = h * 7 + d - 1
            arrived(zs.at[h, 0], zr.at[h, origin], zs_s.at[at], zs_r.at[at], {"pix_0": origin})
            own = own + zr[h, origin].astype(F32)
        pieces[h, c, x, z] = own.astype(BF16)
        piece = pieces.at[h, c, x, z]
        for d in ring:
            at = h * 7 + d - 1
            go(piece, piece, pz_s.at[at], pz_r.at[at], {"pix_0": lax.rem(z + d, 8)})

    def z_gather(h):
        for d in (0,) + ring:
            origin = lax.rem(z + 8 - d, 8)
            piece = pieces.at[h, c, x, origin]
            if d:
                at = h * 7 + d - 1
                arrived(piece, piece, pz_s.at[at], pz_r.at[at], {"pix_0": origin})
            for e in near:
                at = (h * 8 + d) * 3 + e - 1
                go(piece, piece, px_s.at[at], px_r.at[at], {"obs": lax.rem(x + e, 4)})
        group = pieces.at[h, c, x]
        go(group, group, pc_s.at[h * 4], pc_r.at[h * 4], {"pix_1": o})

    def x_gather(h):
        for e in near:
            column = lax.rem(x + 4 - e, 4)
            for d in (0,) + ring:
                at = (h * 8 + d) * 3 + e - 1
                piece = pieces.at[h, c, column, lax.rem(z + 8 - d, 8)]
                arrived(piece, piece, px_s.at[at], px_r.at[at], {"obs": column})
            group = pieces.at[h, c, column]
            go(group, group, pc_s.at[h * 4 + e], pc_r.at[h * 4 + e], {"pix_1": o})

    def core_gather(h):
        for e in (0,) + near:
            group = pieces.at[h, o, lax.rem(x + 4 - e, 4)]
            arrived(group, group, pc_s.at[h * 4 + e], pc_r.at[h * 4 + e], {"pix_1": o})
        for cc in range(2):
            for xx in range(4):
                for zz in range(8):
                    row = cc * core_lines + xx * line + zz * wide
                    result[pl.ds(row, wide), :] = pieces[h, cc, xx, zz].astype(F32)
        out[:, h * SIDE : (h + 1) * SIDE] = result[...].astype(out.dtype)

    fetch(0)
    gather_start(0)
    gather_near(0)
    fetch(1)
    gather_start(1)
    gather_far(0)
    core_sum(0)
    gather_near(1)
    gather_far(1)
    x_sum(0)
    core_sum(1)
    z_sum(0)
    x_sum(1)
    z_gather(0)
    z_sum(1)
    x_gather(0)
    z_gather(1)
    core_gather(0)
    x_gather(1)
    core_gather(1)
    for copy in sends:
        copy.wait_send()


def shards(spectra, enc_weight, pix_tile, pix_local, foot_weight, cotangent, adjoint, mixing):
    rows, features = spectra.shape[0] // 4, cotangent.shape[1]
    channels = spectra.shape[1]
    dma = pltpu.SemaphoreType.DMA
    vmem = pl.BlockSpec(memory_space=pltpu.VMEM)
    anywhere = pl.BlockSpec(memory_space=pl.ANY)
    core, line, wide = channels // 2, channels // 8, channels // 64
    shapes = [
        (enc_weight.shape, BF16),
        ((16, 128), jnp.int32),
        ((16, 128), jnp.int32),
        ((16, 128), F32),
        (adjoint.shape, jnp.int32),
        (mixing.shape, F32),
        (spectra.shape, BF16),
        ((TILE + 256, features), BF16),
        ((2 * TILE + 520, SIDE), F32),
        ((16, SIDE), F32),
        ((8, TILE), jnp.int32),
        ((4 * CAP + 8, SIDE), F32),
        ((4, rows, features), BF16),
        ((4, rows, features), BF16),
        ((2, rows // 2, features), BF16),
        ((16, 1, 128), jnp.int32),
        ((16, 1, 128), jnp.int32),
        None,
        ((rows, 128), F32),
        ((2, 16, CAP, SIDE), BF16),
        ((2, 16, CAP, SIDE), BF16),
        ((rows, features), F32),
        ((rows, 16 * CAP), BF16),
        ((2, rows, SIDE), BF16),
        ((2, 4, rows, SIDE), BF16),
        ((2, SIDE, channels), F32),
        ((2, channels, SIDE), F32),
        ((2, core, SIDE), BF16),
        ((2, core, SIDE), BF16),
        ((2, core, SIDE), F32),
        ((2, 4, line, SIDE), BF16),
        ((2, 4, line, SIDE), BF16),
        ((2, line, SIDE), F32),
        ((2, 8, wide, SIDE), F32),
        ((2, 8, wide, SIDE), BF16),
        ((2, 8, wide, SIDE), BF16),
        ((2, 2, 4, 8, wide, SIDE), BF16),
        ((channels, SIDE), F32),
    ]
    split = shapes.index(None)
    counts = [2, 15, 30, 6, 12, 2, 6, 14, 14, 48, 8]
    encoded = pl.pallas_call(
        whole_kernel,
        out_shape=jax.ShapeDtypeStruct((channels, features), BF16),
        in_specs=[anywhere] * 8,
        out_specs=vmem,
        scratch_shapes=[pltpu.VMEM(*shape) for shape in shapes[:split]]
        + [pltpu.SMEM((16, 1, 128), jnp.int32), pltpu.SMEM((2, 1, 128), jnp.int32)]
        + [pltpu.SMEM((1, TILE), jnp.int32)] * 8
        + [pltpu.VMEM(*shape) for shape in shapes[split + 1 :]]
        + [dma((4,)), dma(()), dma((8,)), dma(()), dma(()), dma((6,))]
        + [dma((n,)) for n in counts for _ in range(2)],
        compiler_params=pltpu.CompilerParams(collective_id=0, has_side_effects=True),
        name="whole",
    )(
        spectra,
        enc_weight,
        pix_tile.reshape(16, 128),
        pix_local.reshape(16, 128),
        foot_weight.reshape(16, 128),
        cotangent,
        adjoint,
        mixing,
    )
    return encoded.astype(F32)


def solution(mesh):
    finer = Mesh(
        mesh.devices.reshape(mesh.shape["obs"], 8, 2, mesh.shape["chan"]),
        ("obs", "pix_0", "pix_1", "chan"),
    )
    placed = (
        P(OBS_PIX, "chan"),
        P("chan", None),
        P(OBS_PIX, None),
        P(OBS_PIX),
        P(OBS_PIX),
        P(PIX, None),
        P(None, PIX),
        P(),
    )
    return jax.shard_map(
        shards, mesh=finer, in_specs=placed, out_specs=P("chan", None), check_vma=False
    )
```

```python
import jax
import jax.numpy as jnp
from jax import lax
from jax.experimental import pallas as pl
from jax.experimental.pallas import tpu as pltpu
from jax.sharding import Mesh
from jax.sharding import PartitionSpec as P

TILE = 4096
CAP = 64
SIDE = 128
STEPS = (4, 3, 5, 2, 6, 1, 7, 0)
PIX = ("pix_0", "pix_1")
OBS_PIX = ("obs", "pix_0", "pix_1")
AXES = ("obs", "pix_0", "pix_1", "chan")
BF16 = jnp.bfloat16
F32 = jnp.float32


def send(source, target, send_sem, recv_sem, where):
    return pltpu.make_async_remote_copy(
        src_ref=source,
        dst_ref=target,
        send_sem=send_sem,
        recv_sem=recv_sem,
        device_id=where,
        device_id_type=pl.DeviceIdType.MESH,
    )


def greet():
    barrier = pltpu.get_barrier_semaphore()
    x, z, c, y = (lax.axis_index(name) for name in AXES)
    peers = [{"obs": lax.rem(x + d, 4)} for d in range(1, 4)]
    peers += [{"chan": lax.rem(y + d, 4)} for d in range(1, 4)]
    for d in range(8):
        for e in range(2):
            if d or e:
                peers.append({"pix_0": lax.rem(z + d, 8), "pix_1": lax.rem(c + e, 2)})
    for peer in peers:
        pl.semaphore_signal(
            barrier, inc=1, device_id=peer, device_id_type=pl.DeviceIdType.MESH
        )
    return barrier, len(peers)


def one_hot(condition):
    return jnp.where(condition, 1.0, 0.0).astype(BF16)


def iota(shape, dim):
    return lax.broadcasted_iota(jnp.int32, shape, dim)


def own_rows(ref, y):
    return jnp.concatenate([ref[pl.ds(4 * y + j, 1), :] for j in range(4)], axis=1)


def ask(tile, local, weight, y, asked, columns):
    tiles, locals_, weights = own_rows(tile, y), own_rows(local, y), own_rows(weight, y)
    rows = tiles.shape[1]
    named = jnp.broadcast_to(tiles, (16, rows)) == iota((16, rows), 0)
    earlier = one_hot(iota((rows, rows), 0) < iota((rows, rows), 1))
    counts = jnp.dot(one_hot(named), earlier, preferred_element_type=F32)
    rank = jnp.sum(jnp.where(named, counts, 0.0), axis=0, keepdims=True)
    placed = one_hot(jnp.broadcast_to(rank, (128, rows)) == iota((128, rows), 0).astype(F32))
    high = lax.shift_right_logical(locals_, 6)
    low = locals_ - high * 64
    wanted = jnp.zeros((16, 128), F32)
    for digit, scale in ((high, 64.0), (low, 1.0)):
        held = jnp.where(named, jnp.broadcast_to(digit.astype(F32), (16, rows)), 0.0).astype(BF16)
        wanted += scale * lax.dot_general(
            held, placed, (((1,), (1,)), ((), ())), preferred_element_type=F32
        )
    for t in range(16):
        asked[t] = jnp.clip(wanted[t : t + 1, :].astype(jnp.int32), 0, TILE - 1)
    slot = tiles.astype(F32) * CAP + rank
    both = jnp.where(iota((128, rows), 0) == 0, jnp.broadcast_to(slot, (128, rows)),
                     jnp.broadcast_to(weights, (128, rows)))
    for j in range(rows // 128):
        block = pl.ds(j * 128, 128)
        columns[block, :] = jnp.transpose(both[:, j * 128 : (j + 1) * 128])


def widen(cot, rows_of, first, count):
    for h in range(2):
        half = cot[pl.ds(first, count), h * SIDE : (h + 1) * SIDE].astype(F32)
        rows_of[pl.ds(2 * first + h, count, stride=2), :] = half


def whole_kernel(spec_hbm, weight_hbm, tile_hbm, local_hbm, foot_hbm, cot_hbm, adjoint_hbm,
                 mixing_hbm, out, weight, tile, local, foot, adjoint, mixing, spec, cot, rows_of, mixed, near_rows, formed, parts, parts_in, relay, asked, asked_in,
                 wanted, chip_wanted, *rest):
    lists, rest = rest[:8], rest[8:]
    (columns, answers, answers_in, slope, chosen, part, shards, total, turned, cs, cr, mine, xs, xr,
                 xsum, zf, zs, zr, pieces, result, ordered, load_sems, cot_sem, list_sems, want_sem,
     chip_sem, in_sems, out_sems,
     halo_s, halo_r, ask_s, ask_r, ans_s, ans_r, rs, rr, gs, gr, core_s, core_r, xs_s, xs_r, zs_s,
     zs_r, pz_s, pz_r, px_s, px_r, pc_s, pc_r) = rest
    x, z, c, y = (lax.axis_index(name) for name in AXES)
    o = 1 - c
    me = z * 2 + c
    rows = part.shape[1]
    right, left, far = lax.rem(y + 1, 4), lax.rem(y + 3, 4), lax.rem(y + 2, 4)
    to_right, to_left = {"chan": right}, {"chan": left}
    lo, hi = pl.ds(0, rows // 2), pl.ds(rows // 2, rows // 2)
    near = (1, 3, 2)
    ring = (1, 7, 2, 6, 3, 5, 4)
    sends = []

    def go(*args):
        copy = send(*args)
        copy.start()
        sends.append(copy)

    finished = [0]

    def drain(upto):
        for copy in sends[finished[0] : upto]:
            copy.wait_send()
        finished[0] = max(upto, finished[0])

    def arrived(*args):
        send(*args).wait_recv()

    barrier, count = greet()
    operands = ((adjoint_hbm, adjoint), (tile_hbm, tile), (local_hbm, local), (foot_hbm, foot),
                (mixing_hbm, mixing), (weight_hbm, weight))
    loads = [pltpu.make_async_copy(a, b, in_sems.at[i]) for i, (a, b) in enumerate(operands)]
    for copy in loads[:5]:
        copy.start()
    cot_copy = pltpu.make_async_copy(cot_hbm, cot.at[pl.ds(128, TILE)], cot_sem)
    cot_copy.start()
    loads[5].start()
    loads[0].wait()
    inside = jnp.clip(adjoint[...] - (me * TILE - SIDE), 0, TILE + 2 * SIDE - 1)
    near_rows[...] = inside * 2
    list_copies = []
    for k in range(8):
        copy = pltpu.make_async_copy(near_rows.at[pl.ds(k, 1)], lists[k], list_sems.at[k])
        copy.start()
        list_copies.append(copy)
    for copy in loads[1:5]:
        copy.wait()
    ask(tile, local, foot, y, asked, columns)
    asked_in[me] = asked[me]
    owners = (far, right, left, y)
    spec_copies = []
    for step, owner in enumerate(owners):
        block = pl.ds(pl.multiple_of(owner * rows, rows), rows)
        copy = pltpu.make_async_copy(spec_hbm.at[block], spec.at[block], load_sems.at[step])
        copy.start()
        spec_copies.append(copy)
    for k in range(8):
        for h in range(2):
            mixed[pl.ds(2 * k + h, 1), :] = mixing[pl.ds(k, 1), h * SIDE : (h + 1) * SIDE]

    order = [(d, e) for d in STEPS for e in (1, 0)]

    def pair(k, ahead):
        d, e = order[k]
        return lax.rem(z + (d if ahead else 8 - d), 8), lax.rem(c + e, 2)

    after = {"pix_0": lax.rem(z + c, 8), "pix_1": o}
    before = {"pix_0": lax.rem(z + 7 + c, 8), "pix_1": o}
    pl.semaphore_wait(barrier, count)
    for k in range(15):
        zz, cc = pair(k, True)
        go(asked.at[zz * 2 + cc], asked_in.at[me], ask_s.at[k], ask_r.at[k],
           {"pix_0": zz, "pix_1": cc})
    ends = cot.at[pl.ds(0, SIDE)], cot.at[pl.ds(TILE + SIDE, SIDE)]
    go(cot_hbm.at[pl.ds(0, SIDE)], ends[1], halo_s.at[0], halo_r.at[0], before)
    go(cot_hbm.at[pl.ds(TILE - SIDE, SIDE)], ends[0], halo_s.at[1], halo_r.at[1], after)

    cot_copy.wait()

    def widen_step(i, carry):
        widen(cot, rows_of, pl.multiple_of(SIDE + i * 256, SIDE), 256)
        return carry

    lax.fori_loop(0, TILE // 256, widen_step, 0)

    loads[5].wait()

    def encode(step):
        owner = owners[step]
        spec_copies[step].wait()
        block = spec[pl.ds(pl.multiple_of(owner * rows, rows), rows), :]
        parts[owner] = jnp.dot(block, weight[...], preferred_element_type=F32).astype(BF16)

    encode(0)
    go(parts.at[far, lo], relay.at[0], rs.at[0], rr.at[0], to_right)
    go(parts.at[far, hi], relay.at[1], rs.at[1], rr.at[1], to_left)
    encode(1)
    go(parts.at[right], parts_in.at[y], rs.at[2], rr.at[2], to_right)
    encode(2)
    go(parts.at[left], parts_in.at[y], rs.at[3], rr.at[3], to_left)
    arrived(cot_hbm.at[pl.ds(0, SIDE)], ends[1], halo_s.at[0], halo_r.at[0], after)
    arrived(cot_hbm.at[pl.ds(0, SIDE)], ends[0], halo_s.at[1], halo_r.at[1], before)
    widen(cot, rows_of, 0, SIDE)
    widen(cot, rows_of, TILE + SIDE, SIDE)
    for copy in list_copies:
        copy.wait()

    def requested(k):
        zz, cc = pair(k, False)
        arrived(asked.at[0], asked_in.at[zz * 2 + cc], ask_s.at[k], ask_r.at[k],
                {"pix_0": zz, "pix_1": cc})

    def serve(k, source):
        zz, cc = pair(k, False)
        asker = zz * 2 + cc
        mix = [mixed[pl.ds(2 * n, 2), :] for n in range(8)]
        unroll = 32

        def some(i, carry):
            for u in range(unroll):
                at = i * unroll + u
                pixel = source[asker if source is wanted else cc, 0, at]
                row = rows_of[pl.ds(pixel * 2 + 2 * SIDE, 2), :]
                for n in range(8):
                    row = row + rows_of[pl.ds(lists[n][0, pixel], 2), :] * mix[n]
                formed[pl.ds(k % 2 * 2 * CAP + 2 * at, 2), :] = row
            return carry

        lax.fori_loop(0, CAP // unroll, some, 0)
        for h in range(2):
            half = formed[pl.ds(k % 2 * 2 * CAP + h, CAP, stride=2), :]
            answers[h, k] = half.astype(BF16)

    def reply(h, k):
        zz, cc = pair(k, False)
        go(answers.at[h, k], answers_in.at[h, me], ans_s.at[h * 15 + k], ans_r.at[h * 15 + k],
           {"pix_0": zz, "pix_1": cc})

    requested(14)
    chip_copy = pltpu.make_async_copy(asked_in.at[pl.ds(2 * z, 2)], chip_wanted, chip_sem)
    chip_copy.start()
    chip_copy.wait()
    serve(15, chip_wanted)
    serve(14, chip_wanted)
    reply(0, 14)
    for h in range(2):
        answers_in[h, me] = answers[h, 15]
    for k in range(14):
        requested(k)
    want_copy = pltpu.make_async_copy(asked_in, wanted, want_sem)
    want_copy.start()
    want_copy.wait()
    lag = 10
    for k in range(14):
        serve(k, wanted)
        reply(0, k)
        if k == 0:
            reply(1, 14)
        if k >= lag:
            reply(1, k - lag)
        if k == 0:
            arrived(parts.at[far, lo], relay.at[0], rs.at[0], rr.at[0], to_left)
            go(relay.at[0], parts_in.at[left, lo], rs.at[4], rr.at[4], to_right)
            arrived(parts.at[far, hi], relay.at[1], rs.at[1], rr.at[1], to_right)
            go(relay.at[1], parts_in.at[right, hi], rs.at[5], rr.at[5], to_left)
    for k in range(14 - lag, 14):
        reply(1, k)
    encode(3)

    slots = 16 * CAP
    chosen[...] = one_hot(
        jnp.broadcast_to(columns[:, 0:1], (rows, slots)) == iota((rows, slots), 1).astype(F32)
    )
    arrived(parts.at[0], parts_in.at[left], rs.at[2], rr.at[2], to_left)
    arrived(parts.at[0], parts_in.at[right], rs.at[3], rr.at[3], to_right)
    arrived(relay.at[0], parts_in.at[far, lo], rs.at[4], rr.at[4], to_left)
    arrived(relay.at[1], parts_in.at[far, hi], rs.at[5], rr.at[5], to_right)
    pre = parts[y].astype(F32)
    for origin in (left, right, far):
        pre = pre + parts_in[origin].astype(F32)
    sigma = 1.0 / (1.0 + jnp.exp(-pre))
    slope[...] = columns[:, 1:2] * (sigma * (1.0 + pre * (1.0 - sigma)))

    def fetch(h):
        for k in range(15):
            zz, cc = pair(k, True)
            arrived(answers.at[h, k], answers_in.at[h, zz * 2 + cc], ans_s.at[h * 15 + k],
                    ans_r.at[h * 15 + k], {"pix_0": zz, "pix_1": cc})
        rows_in = answers_in[h].reshape(slots, SIDE)
        fetched = jnp.dot(chosen[...], rows_in, preferred_element_type=F32)
        part[h] = (slope[:, h * SIDE : (h + 1) * SIDE] * fetched).astype(BF16)

    def multiply(h, gradient, owner, fresh=False):
        flat = jnp.transpose(gradient.astype(F32)).astype(BF16)
        width = spec.shape[1] // 3
        for n in range(3):
            cols = pl.ds(n * width, width)
            block = spec[pl.ds(pl.multiple_of(owner * rows, rows), rows), cols]
            product = jnp.dot(flat, block, preferred_element_type=F32)
            if fresh:
                total[h, :, cols] = product
            else:
                total[h, :, cols] += product

    def gather_start(h):
        i = h * 6
        mine_, store = part.at[h], shards.at[h]
        go(mine_.at[lo], store.at[y, lo], gs.at[i], gr.at[i], to_right)
        go(mine_.at[hi], store.at[y, hi], gs.at[i + 1], gr.at[i + 1], to_left)
        multiply(h, part[h], y, True)
        go(mine_.at[hi], store.at[y, hi], gs.at[i + 2], gr.at[i + 2], to_right)
        go(mine_.at[lo], store.at[y, lo], gs.at[i + 3], gr.at[i + 3], to_left)

    def gather_near(h):
        i = h * 6
        mine_, store = part.at[h], shards.at[h]
        arrived(mine_.at[lo], store.at[left, lo], gs.at[i], gr.at[i], to_left)
        go(store.at[left, lo], store.at[left, lo], gs.at[i + 4], gr.at[i + 4], to_right)
        arrived(mine_.at[hi], store.at[right, hi], gs.at[i + 1], gr.at[i + 1], to_right)
        go(store.at[right, hi], store.at[right, hi], gs.at[i + 5], gr.at[i + 5], to_left)
        arrived(mine_.at[hi], store.at[left, hi], gs.at[i + 2], gr.at[i + 2], to_left)
        multiply(h, shards[h, left], left)
        arrived(mine_.at[lo], store.at[right, lo], gs.at[i + 3], gr.at[i + 3], to_right)
        multiply(h, shards[h, right], right)

    core_lines, line, wide = mine.shape[1], xs.shape[2], zs.shape[2]

    def gather_far(h):
        i = h * 6
        store = shards.at[h]
        arrived(store.at[far, lo], store.at[far, lo], gs.at[i + 4], gr.at[i + 4], to_left)
        arrived(store.at[far, hi], store.at[far, hi], gs.at[i + 5], gr.at[i + 5], to_right)
        multiply(h, shards[h, far], far)
        for j in range(total.shape[2] // SIDE):
            block = pl.ds(j * SIDE, SIDE)
            turned[h, block, :] = jnp.transpose(total[h, :, block])
        theirs = pl.ds(pl.multiple_of(o * core_lines, 8), core_lines)
        cs[h] = turned[h, theirs, :].astype(BF16)
        go(cs.at[h], cr.at[h], core_s.at[h], core_r.at[h], {"pix_1": o})

    def core_sum(h):
        arrived(cs.at[h], cr.at[h], core_s.at[h], core_r.at[h], {"pix_1": o})
        ours = pl.ds(pl.multiple_of(c * core_lines, 8), core_lines)
        mine[h] = turned[h, ours, :] + cr[h].astype(F32)
        for j in range(4):
            xs[h, j] = mine[h, pl.ds(j * line, line), :].astype(BF16)
        for d in near:
            peer = lax.rem(x + d, 4)
            at = h * 3 + d - 1
            go(xs.at[h, peer], xr.at[h, x], xs_s.at[at], xs_r.at[at], {"obs": peer})

    def x_sum(h):
        summed = mine[h, pl.ds(pl.multiple_of(x * line, 8), line), :]
        for d in near:
            origin = lax.rem(x + 4 - d, 4)
            at = h * 3 + d - 1
            arrived(xs.at[h, 0], xr.at[h, origin], xs_s.at[at], xs_r.at[at], {"obs": origin})
            summed = summed + xr[h, origin].astype(F32)
        xsum[h] = summed
        for j in range(8):
            zf[h, j] = xsum[h, pl.ds(j * wide, wide), :]
            zs[h, j] = zf[h, j].astype(BF16)
        for d in ring:
            peer = lax.rem(z + d, 8)
            at = h * 7 + d - 1
            go(zs.at[h, peer], zr.at[h, z], zs_s.at[at], zs_r.at[at], {"pix_0": peer})

    def z_sum(h):
        own = zf[h, z]
        for d in ring:
            origin = lax.rem(z + 8 - d, 8)
            at = h * 7 + d - 1
            arrived(zs.at[h, 0], zr.at[h, origin], zs_s.at[at], zs_r.at[at], {"pix_0": origin})
            own = own + zr[h, origin].astype(F32)
        pieces[h, c, x, z] = own.astype(BF16)
        piece = pieces.at[h, c, x, z]
        for d in ring:
            at = h * 7 + d - 1
            go(piece, piece, pz_s.at[at], pz_r.at[at], {"pix_0": lax.rem(z + d, 8)})

    def z_gather(h):
        for d in (0,) + ring:
            origin = lax.rem(z + 8 - d, 8)
            piece = pieces.at[h, c, x, origin]
            if d:
                at = h * 7 + d - 1
                arrived(piece, piece, pz_s.at[at], pz_r.at[at], {"pix_0": origin})
            for e in near:
                at = (h * 8 + d) * 3 + e - 1
                go(piece, piece, px_s.at[at], px_r.at[at], {"obs": lax.rem(x + e, 4)})
        group = pieces.at[h, c, x]
        go(group, group, pc_s.at[h * 4], pc_r.at[h * 4], {"pix_1": o})

    def assemble(h, core):
        for xx in range(4):
            for zz in range(8):
                row = xx * line + zz * wide
                result[core, pl.ds(row, wide), :] = pieces[h, core, xx, zz].astype(F32)
        ordered[h, core] = result[core].astype(BF16)
        target = out.at[pl.ds(pl.multiple_of(core * core_lines, 8), core_lines),
                        pl.ds(h * SIDE, SIDE)]
        copy = pltpu.make_async_copy(ordered.at[h, core], target, out_sems.at[len(results)])
        copy.start()
        results.append(copy)

    results = []

    def x_gather(h):
        for e in near:
            column = lax.rem(x + 4 - e, 4)
            for d in (0,) + ring:
                at = (h * 8 + d) * 3 + e - 1
                piece = pieces.at[h, c, column, lax.rem(z + 8 - d, 8)]
                arrived(piece, piece, px_s.at[at], px_r.at[at], {"obs": column})
            group = pieces.at[h, c, column]
            go(group, group, pc_s.at[h * 4 + e], pc_r.at[h * 4 + e], {"pix_1": o})
        assemble(h, c)

    def core_gather(h):
        for e in (0,) + near:
            group = pieces.at[h, o, lax.rem(x + 4 - e, 4)]
            arrived(group, group, pc_s.at[h * 4 + e], pc_r.at[h * 4 + e], {"pix_1": o})
        assemble(h, o)

    fetch(0)
    gather_start(0)
    gather_near(0)
    fetch(1)
    gather_start(1)
    gather_far(0)
    core_sum(0)
    gather_near(1)
    gathered = len(sends)
    gather_far(1)
    x_sum(0)
    core_sum(1)
    x_sent = len(sends)
    drain(gathered)
    z_sum(0)
    x_sum(1)
    z_sent = len(sends)
    drain(x_sent)
    z_gather(0)
    z_sum(1)
    first_sent = len(sends)
    drain(z_sent)
    x_gather(0)
    z_gather(1)
    core_gather(0)
    drain(first_sent)
    x_gather(1)
    core_gather(1)
    drain(len(sends))
    for copy in results:
        copy.wait()


def shards(spectra, enc_weight, pix_tile, pix_local, foot_weight, cotangent, adjoint, mixing):
    rows, features = spectra.shape[0] // 4, cotangent.shape[1]
    channels = spectra.shape[1]
    dma = pltpu.SemaphoreType.DMA
    anywhere = pl.BlockSpec(memory_space=pl.ANY)
    core, line, wide = channels // 2, channels // 8, channels // 64
    shapes = [
        (enc_weight.shape, BF16),
        ((16, 128), jnp.int32),
        ((16, 128), jnp.int32),
        ((16, 128), F32),
        (adjoint.shape, jnp.int32),
        (mixing.shape, F32),
        (spectra.shape, BF16),
        ((TILE + 256, features), BF16),
        ((2 * TILE + 520, SIDE), F32),
        ((16, SIDE), F32),
        ((8, TILE), jnp.int32),
        ((4 * CAP + 8, SIDE), F32),
        ((4, rows, features), BF16),
        ((4, rows, features), BF16),
        ((2, rows // 2, features), BF16),
        ((16, 1, 128), jnp.int32),
        ((16, 1, 128), jnp.int32),
        None,
        ((rows, 128), F32),
        ((2, 16, CAP, SIDE), BF16),
        ((2, 16, CAP, SIDE), BF16),
        ((rows, features), F32),
        ((rows, 16 * CAP), BF16),
        ((2, rows, SIDE), BF16),
        ((2, 4, rows, SIDE), BF16),
        ((2, SIDE, channels), F32),
        ((2, channels, SIDE), F32),
        ((2, core, SIDE), BF16),
        ((2, core, SIDE), BF16),
        ((2, core, SIDE), F32),
        ((2, 4, line, SIDE), BF16),
        ((2, 4, line, SIDE), BF16),
        ((2, line, SIDE), F32),
        ((2, 8, wide, SIDE), F32),
        ((2, 8, wide, SIDE), BF16),
        ((2, 8, wide, SIDE), BF16),
        ((2, 2, 4, 8, wide, SIDE), BF16),
        ((2, core, SIDE), F32),
        ((2, 2, core, SIDE), BF16),
    ]
    split = shapes.index(None)
    counts = [2, 15, 30, 6, 12, 2, 6, 14, 14, 48, 8]
    encoded = pl.pallas_call(
        whole_kernel,
        out_shape=jax.ShapeDtypeStruct((channels, features), BF16),
        in_specs=[anywhere] * 8,
        out_specs=anywhere,
        scratch_shapes=[pltpu.VMEM(*shape) for shape in shapes[:split]]
        + [pltpu.SMEM((16, 1, 128), jnp.int32), pltpu.SMEM((2, 1, 128), jnp.int32)]
        + [pltpu.SMEM((1, TILE), jnp.int32)] * 8
        + [pltpu.VMEM(*shape) for shape in shapes[split + 1 :]]
        + [dma((4,)), dma(()), dma((8,)), dma(()), dma(()), dma((6,)), dma((4,))]
        + [dma((n,)) for n in counts for _ in range(2)],
        compiler_params=pltpu.CompilerParams(collective_id=0, has_side_effects=True),
        name="whole",
    )(
        spectra,
        enc_weight,
        pix_tile.reshape(16, 128),
        pix_local.reshape(16, 128),
        foot_weight.reshape(16, 128),
        cotangent,
        adjoint,
        mixing,
    )
    return encoded.astype(F32)


def solution(mesh):
    finer = Mesh(
        mesh.devices.reshape(mesh.shape["obs"], 8, 2, mesh.shape["chan"]),
        ("obs", "pix_0", "pix_1", "chan"),
    )
    placed = (
        P(OBS_PIX, "chan"),
        P("chan", None),
        P(OBS_PIX, None),
        P(OBS_PIX),
        P(OBS_PIX),
        P(PIX, None),
        P(None, PIX),
        P(),
    )
    return jax.shard_map(
        shards, mesh=finer, in_specs=placed, out_specs=P("chan", None), check_vma=False
    )
```

```python
import jax
import jax.numpy as jnp
from jax import lax
from jax.experimental import pallas as pl
from jax.experimental.pallas import tpu as pltpu
from jax.sharding import Mesh
from jax.sharding import PartitionSpec as P

TILE = 4096
CAP = 64
SIDE = 128
STEPS = (4, 3, 5, 2, 6, 1, 7, 0)
PIX = ("pix_0", "pix_1")
OBS_PIX = ("obs", "pix_0", "pix_1")
AXES = ("obs", "pix_0", "pix_1", "chan")
BF16 = jnp.bfloat16
F32 = jnp.float32


def send(source, target, send_sem, recv_sem, where):
    return pltpu.make_async_remote_copy(
        src_ref=source,
        dst_ref=target,
        send_sem=send_sem,
        recv_sem=recv_sem,
        device_id=where,
        device_id_type=pl.DeviceIdType.MESH,
    )


def greet():
    barrier = pltpu.get_barrier_semaphore()
    x, z, c, y = (lax.axis_index(name) for name in AXES)
    peers = [{"obs": lax.rem(x + d, 4)} for d in range(1, 4)]
    peers += [{"chan": lax.rem(y + d, 4)} for d in range(1, 4)]
    for d in range(8):
        for e in range(2):
            if d or e:
                peers.append({"pix_0": lax.rem(z + d, 8), "pix_1": lax.rem(c + e, 2)})
    for peer in peers:
        pl.semaphore_signal(
            barrier, inc=1, device_id=peer, device_id_type=pl.DeviceIdType.MESH
        )
    return barrier, len(peers)


def one_hot(condition):
    return jnp.where(condition, 1.0, 0.0).astype(BF16)


def iota(shape, dim):
    return lax.broadcasted_iota(jnp.int32, shape, dim)


def own_rows(ref, y):
    return jnp.concatenate([ref[pl.ds(4 * y + j, 1), :] for j in range(4)], axis=1)


def ask(tile, local, weight, y, asked, columns):
    tiles, locals_, weights = own_rows(tile, y), own_rows(local, y), own_rows(weight, y)
    rows = tiles.shape[1]
    named = jnp.broadcast_to(tiles, (16, rows)) == iota((16, rows), 0)
    earlier = one_hot(iota((rows, rows), 0) < iota((rows, rows), 1))
    counts = jnp.dot(one_hot(named), earlier, preferred_element_type=F32)
    rank = jnp.sum(jnp.where(named, counts, 0.0), axis=0, keepdims=True)
    placed = one_hot(jnp.broadcast_to(rank, (128, rows)) == iota((128, rows), 0).astype(F32))
    high = lax.shift_right_logical(locals_, 6)
    low = locals_ - high * 64
    wanted = jnp.zeros((16, 128), F32)
    for digit, scale in ((high, 64.0), (low, 1.0)):
        held = jnp.where(named, jnp.broadcast_to(digit.astype(F32), (16, rows)), 0.0).astype(BF16)
        wanted += scale * lax.dot_general(
            held, placed, (((1,), (1,)), ((), ())), preferred_element_type=F32
        )
    for t in range(16):
        asked[t] = jnp.clip(wanted[t : t + 1, :].astype(jnp.int32), 0, TILE - 1)
    slot = tiles.astype(F32) * CAP + rank
    both = jnp.where(iota((128, rows), 0) == 0, jnp.broadcast_to(slot, (128, rows)),
                     jnp.broadcast_to(weights, (128, rows)))
    for j in range(rows // 128):
        block = pl.ds(j * 128, 128)
        columns[block, :] = jnp.transpose(both[:, j * 128 : (j + 1) * 128])


def widen(cot, rows_of, first, count):
    for h in range(2):
        half = cot[pl.ds(first, count), h * SIDE : (h + 1) * SIDE].astype(F32)
        rows_of[pl.ds(2 * first + h, count, stride=2), :] = half


def whole_kernel(spec_hbm, weight_hbm, tile_hbm, local_hbm, foot_hbm, cot_hbm, adjoint_hbm,
                 mixing_hbm, out, weight, tile, local, foot, adjoint, mixing, spec, cot, rows_of, mixed, near_rows, formed, parts, parts_in, relay, asked, asked_in,
                 wanted, chip_wanted, *rest):
    lists, rest = rest[:8], rest[8:]
    (columns, answers, answers_in, slope, chosen, part, shards, total, turned, cs, cr, mine, xs, xr,
                 xsum, zf, zs, zr, pieces, result, ordered, load_sems, cot_sem, list_sems, want_sem,
     chip_sem, in_sems, out_sems,
     halo_s, halo_r, ask_s, ask_r, ans_s, ans_r, rs, rr, gs, gr, core_s, core_r, xs_s, xs_r, zs_s,
     zs_r, pz_s, pz_r, px_s, px_r, pc_s, pc_r) = rest
    x, z, c, y = (lax.axis_index(name) for name in AXES)
    o = 1 - c
    me = z * 2 + c
    rows = part.shape[1]
    right, left, far = lax.rem(y + 1, 4), lax.rem(y + 3, 4), lax.rem(y + 2, 4)
    to_right, to_left = {"chan": right}, {"chan": left}
    lo, hi = pl.ds(0, rows // 2), pl.ds(rows // 2, rows // 2)
    near = (1, 3, 2)
    ring = (1, 7, 2, 6, 3, 5, 4)
    sibling = {"pix_1": o}

    def go(*args):
        send(*args).start()

    def landed(ref, sem):
        send(ref, ref, sem, sem, sibling).wait_recv()

    def gone(ref, sem):
        send(ref, ref, sem, sem, sibling).wait_send()

    barrier, count = greet()
    operands = ((adjoint_hbm, adjoint), (tile_hbm, tile), (local_hbm, local), (foot_hbm, foot),
                (mixing_hbm, mixing), (weight_hbm, weight))
    loads = [pltpu.make_async_copy(a, b, in_sems.at[i]) for i, (a, b) in enumerate(operands)]
    for copy in loads[:5]:
        copy.start()
    cot_copy = pltpu.make_async_copy(cot_hbm, cot.at[pl.ds(128, TILE)], cot_sem)
    cot_copy.start()
    loads[5].start()
    loads[0].wait()
    inside = jnp.clip(adjoint[...] - (me * TILE - SIDE), 0, TILE + 2 * SIDE - 1)
    near_rows[...] = inside * 2
    list_copies = []
    for k in range(8):
        copy = pltpu.make_async_copy(near_rows.at[pl.ds(k, 1)], lists[k], list_sems.at[k])
        copy.start()
        list_copies.append(copy)
    for copy in loads[1:5]:
        copy.wait()
    ask(tile, local, foot, y, asked, columns)
    asked_in[me] = asked[me]
    owners = (far, right, left, y)
    spec_copies = []
    for step, owner in enumerate(owners):
        block = pl.ds(pl.multiple_of(owner * rows, rows), rows)
        copy = pltpu.make_async_copy(spec_hbm.at[block], spec.at[block], load_sems.at[step])
        copy.start()
        spec_copies.append(copy)
    for k in range(8):
        for h in range(2):
            mixed[pl.ds(2 * k + h, 1), :] = mixing[pl.ds(k, 1), h * SIDE : (h + 1) * SIDE]

    order = [(d, e) for d in STEPS for e in (1, 0)]

    def pair(k, ahead):
        d, e = order[k]
        return lax.rem(z + (d if ahead else 8 - d), 8), lax.rem(c + e, 2)

    after = {"pix_0": lax.rem(z + c, 8), "pix_1": o}
    before = {"pix_0": lax.rem(z + 7 + c, 8), "pix_1": o}
    pl.semaphore_wait(barrier, count)
    for k in range(15):
        zz, cc = pair(k, True)
        go(asked.at[zz * 2 + cc], asked_in.at[me], ask_s.at[0], ask_r.at[k // 14],
           {"pix_0": zz, "pix_1": cc})
    ends = cot.at[pl.ds(0, SIDE)], cot.at[pl.ds(TILE + SIDE, SIDE)]
    go(cot_hbm.at[pl.ds(0, SIDE)], ends[1], halo_s.at[0], halo_r.at[0], before)
    go(cot_hbm.at[pl.ds(TILE - SIDE, SIDE)], ends[0], halo_s.at[0], halo_r.at[0], after)

    cot_copy.wait()

    def widen_step(i, carry):
        widen(cot, rows_of, pl.multiple_of(SIDE + i * 256, SIDE), 256)
        return carry

    lax.fori_loop(0, TILE // 256, widen_step, 0)

    loads[5].wait()

    def encode(step):
        owner = owners[step]
        spec_copies[step].wait()
        block = spec[pl.ds(pl.multiple_of(owner * rows, rows), rows), :]
        parts[owner] = jnp.dot(block, weight[...], preferred_element_type=F32).astype(BF16)

    encode(0)
    go(parts.at[far, lo], relay.at[0], rs.at[0], rr.at[0], to_right)
    go(parts.at[far, hi], relay.at[1], rs.at[0], rr.at[1], to_left)
    encode(1)
    go(parts.at[right], parts_in.at[y], rs.at[0], rr.at[2], to_right)
    encode(2)
    go(parts.at[left], parts_in.at[y], rs.at[0], rr.at[2], to_left)
    landed(cot.at[pl.ds(0, 2 * SIDE)], halo_r.at[0])
    widen(cot, rows_of, 0, SIDE)
    widen(cot, rows_of, TILE + SIDE, SIDE)
    for copy in list_copies:
        copy.wait()

    def serve(k, source):
        zz, cc = pair(k, False)
        asker = zz * 2 + cc
        mix = [mixed[pl.ds(2 * n, 2), :] for n in range(8)]
        unroll = 32

        def some(i, carry):
            for u in range(unroll):
                at = i * unroll + u
                pixel = source[asker if source is wanted else cc, 0, at]
                row = rows_of[pl.ds(pixel * 2 + 2 * SIDE, 2), :]
                for n in range(8):
                    row = row + rows_of[pl.ds(lists[n][0, pixel], 2), :] * mix[n]
                formed[pl.ds(k % 2 * 2 * CAP + 2 * at, 2), :] = row
            return carry

        lax.fori_loop(0, CAP // unroll, some, 0)
        for h in range(2):
            half = formed[pl.ds(k % 2 * 2 * CAP + h, CAP, stride=2), :]
            answers[h, k] = half.astype(BF16)

    def reply(h, k):
        zz, cc = pair(k, False)
        go(answers.at[h, k], answers_in.at[h, me], ans_s.at[h], ans_r.at[h],
           {"pix_0": zz, "pix_1": cc})

    landed(asked_in.at[0], ask_r.at[1])
    chip_copy = pltpu.make_async_copy(asked_in.at[pl.ds(2 * z, 2)], chip_wanted, chip_sem)
    chip_copy.start()
    chip_copy.wait()
    serve(15, chip_wanted)
    serve(14, chip_wanted)
    reply(0, 14)
    for h in range(2):
        answers_in[h, me] = answers[h, 15]
    landed(asked_in.at[pl.ds(0, 14)], ask_r.at[0])
    want_copy = pltpu.make_async_copy(asked_in, wanted, want_sem)
    want_copy.start()
    want_copy.wait()
    lag = 10
    for k in range(14):
        serve(k, wanted)
        reply(0, k)
        if k == 0:
            reply(1, 14)
        if k >= lag:
            reply(1, k - lag)
        if k == 0:
            landed(relay.at[0], rr.at[0])
            go(relay.at[0], parts_in.at[left, lo], rs.at[0], rr.at[2], to_right)
            landed(relay.at[1], rr.at[1])
            go(relay.at[1], parts_in.at[right, hi], rs.at[0], rr.at[2], to_left)
    for k in range(14 - lag, 14):
        reply(1, k)
    encode(3)

    slots = 16 * CAP
    chosen[...] = one_hot(
        jnp.broadcast_to(columns[:, 0:1], (rows, slots)) == iota((rows, slots), 1).astype(F32)
    )
    landed(parts_in.at[pl.ds(0, 3)], rr.at[2])
    pre = parts[y].astype(F32)
    for origin in (left, right, far):
        pre = pre + parts_in[origin].astype(F32)
    sigma = 1.0 / (1.0 + jnp.exp(-pre))
    slope[...] = columns[:, 1:2] * (sigma * (1.0 + pre * (1.0 - sigma)))

    def fetch(h):
        landed(answers_in.at[h, pl.ds(0, 15)], ans_r.at[h])
        rows_in = answers_in[h].reshape(slots, SIDE)
        fetched = jnp.dot(chosen[...], rows_in, preferred_element_type=F32)
        part[h] = (slope[:, h * SIDE : (h + 1) * SIDE] * fetched).astype(BF16)

    def multiply(h, gradient, owner, fresh=False):
        flat = jnp.transpose(gradient.astype(F32)).astype(BF16)
        width = spec.shape[1] // 3
        for n in range(3):
            cols = pl.ds(n * width, width)
            block = spec[pl.ds(pl.multiple_of(owner * rows, rows), rows), cols]
            product = jnp.dot(flat, block, preferred_element_type=F32)
            if fresh:
                total[h, :, cols] = product
            else:
                total[h, :, cols] += product

    def gather_start(h):
        i = h * 6
        mine_, store = part.at[h], shards.at[h]
        go(mine_.at[lo], store.at[y, lo], gs.at[h], gr.at[i], to_right)
        go(mine_.at[hi], store.at[y, hi], gs.at[h], gr.at[i + 1], to_left)
        multiply(h, part[h], y, True)
        go(mine_.at[hi], store.at[y, hi], gs.at[h], gr.at[i + 2], to_right)
        go(mine_.at[lo], store.at[y, lo], gs.at[h], gr.at[i + 3], to_left)

    def gather_near(h):
        i = h * 6
        mine_, store = part.at[h], shards.at[h]
        landed(store.at[left, lo], gr.at[i])
        go(store.at[left, lo], store.at[left, lo], gs.at[h], gr.at[i + 4], to_right)
        landed(store.at[right, hi], gr.at[i + 1])
        go(store.at[right, hi], store.at[right, hi], gs.at[h], gr.at[i + 5], to_left)
        landed(store.at[left, hi], gr.at[i + 2])
        multiply(h, shards[h, left], left)
        landed(store.at[right, lo], gr.at[i + 3])
        multiply(h, shards[h, right], right)

    core_lines, line, wide = mine.shape[1], xs.shape[2], zs.shape[2]

    def gather_far(h):
        i = h * 6
        store = shards.at[h]
        landed(store.at[far, lo], gr.at[i + 4])
        landed(store.at[far, hi], gr.at[i + 5])
        multiply(h, shards[h, far], far)
        for j in range(total.shape[2] // SIDE):
            block = pl.ds(j * SIDE, SIDE)
            turned[h, block, :] = jnp.transpose(total[h, :, block])
        theirs = pl.ds(pl.multiple_of(o * core_lines, 8), core_lines)
        cs[h] = turned[h, theirs, :].astype(BF16)
        go(cs.at[h], cr.at[h], core_s.at[h], core_r.at[h], {"pix_1": o})

    def core_sum(h):
        landed(cr.at[h], core_r.at[h])
        ours = pl.ds(pl.multiple_of(c * core_lines, 8), core_lines)
        mine[h] = turned[h, ours, :] + cr[h].astype(F32)
        for j in range(4):
            xs[h, j] = mine[h, pl.ds(j * line, line), :].astype(BF16)
        for d in near:
            peer = lax.rem(x + d, 4)
            go(xs.at[h, peer], xr.at[h, x], xs_s.at[h], xs_r.at[h], {"obs": peer})

    def x_sum(h):
        summed = mine[h, pl.ds(pl.multiple_of(x * line, 8), line), :]
        landed(xr.at[h, pl.ds(0, 3)], xs_r.at[h])
        for d in near:
            summed = summed + xr[h, lax.rem(x + 4 - d, 4)].astype(F32)
        xsum[h] = summed
        for j in range(8):
            zf[h, j] = xsum[h, pl.ds(j * wide, wide), :]
            zs[h, j] = zf[h, j].astype(BF16)
        for d in ring:
            peer = lax.rem(z + d, 8)
            go(zs.at[h, peer], zr.at[h, z], zs_s.at[h], zs_r.at[h], {"pix_0": peer})

    def z_sum(h):
        own = zf[h, z]
        landed(zr.at[h, pl.ds(0, 7)], zs_r.at[h])
        for d in ring:
            own = own + zr[h, lax.rem(z + 8 - d, 8)].astype(F32)
        pieces[h, c, x, z] = own.astype(BF16)
        piece = pieces.at[h, c, x, z]
        for d in ring:
            at = h * 7 + d - 1
            go(piece, piece, pz_s.at[h], pz_r.at[at], {"pix_0": lax.rem(z + d, 8)})

    def z_gather(h):
        for d in (0,) + ring:
            origin = lax.rem(z + 8 - d, 8)
            piece = pieces.at[h, c, x, origin]
            if d:
                landed(piece, pz_r.at[h * 7 + d - 1])
            for e in near:
                at = h * 3 + e - 1
                go(piece, piece, px_s.at[h], px_r.at[at], {"obs": lax.rem(x + e, 4)})
        group = pieces.at[h, c, x]
        go(group, group, pc_s.at[h], pc_r.at[h], {"pix_1": o})

    def assemble(h, core):
        for xx in range(4):
            for zz in range(8):
                row = xx * line + zz * wide
                result[core, pl.ds(row, wide), :] = pieces[h, core, xx, zz].astype(F32)
        ordered[h, core] = result[core].astype(BF16)
        target = out.at[pl.ds(pl.multiple_of(core * core_lines, 8), core_lines),
                        pl.ds(h * SIDE, SIDE)]
        copy = pltpu.make_async_copy(ordered.at[h, core], target, out_sems.at[len(results)])
        copy.start()
        results.append(copy)

    results = []

    def x_gather(h):
        for e in near:
            column = lax.rem(x + 4 - e, 4)
            group = pieces.at[h, c, column]
            landed(group, px_r.at[h * 3 + e - 1])
            go(group, group, pc_s.at[h], pc_r.at[h], {"pix_1": o})
        assemble(h, c)

    def core_gather(h):
        landed(pieces.at[h, o], pc_r.at[h])
        assemble(h, o)

    fetch(0)
    gather_start(0)
    gather_near(0)
    fetch(1)
    gather_start(1)
    gather_far(0)
    core_sum(0)
    gather_near(1)
    gather_far(1)
    x_sum(0)
    core_sum(1)
    gone(asked.at[pl.ds(0, 15)], ask_s.at[0])
    gone(cot.at[pl.ds(0, 2 * SIDE)], halo_s.at[0])
    gone(parts, rs.at[0])
    for h in range(2):
        gone(answers.at[h, pl.ds(0, 15)], ans_s.at[h])
        gone(shards.at[h, pl.ds(0, 3)], gs.at[h])
    z_sum(0)
    x_sum(1)
    for h in range(2):
        gone(cs.at[h], core_s.at[h])
        gone(xs.at[h, pl.ds(0, 3)], xs_s.at[h])
    z_gather(0)
    z_sum(1)
    for h in range(2):
        gone(zs.at[h, pl.ds(0, 7)], zs_s.at[h])
    x_gather(0)
    z_gather(1)
    core_gather(0)
    for h in range(2):
        gone(pieces.at[h, 0, 0, pl.ds(0, 7)], pz_s.at[h])
    gone(pieces.at[0, 0, pl.ds(0, 3)], px_s.at[0])
    x_gather(1)
    core_gather(1)
    gone(pieces.at[1, 0, pl.ds(0, 3)], px_s.at[1])
    for h in range(2):
        gone(pieces.at[h, 0], pc_s.at[h])
    for copy in results:
        copy.wait()


def shards(spectra, enc_weight, pix_tile, pix_local, foot_weight, cotangent, adjoint, mixing):
    rows, features = spectra.shape[0] // 4, cotangent.shape[1]
    channels = spectra.shape[1]
    dma = pltpu.SemaphoreType.DMA
    anywhere = pl.BlockSpec(memory_space=pl.ANY)
    core, line, wide = channels // 2, channels // 8, channels // 64
    shapes = [
        (enc_weight.shape, BF16),
        ((16, 128), jnp.int32),
        ((16, 128), jnp.int32),
        ((16, 128), F32),
        (adjoint.shape, jnp.int32),
        (mixing.shape, F32),
        (spectra.shape, BF16),
        ((TILE + 256, features), BF16),
        ((2 * TILE + 520, SIDE), F32),
        ((16, SIDE), F32),
        ((8, TILE), jnp.int32),
        ((4 * CAP + 8, SIDE), F32),
        ((4, rows, features), BF16),
        ((4, rows, features), BF16),
        ((2, rows // 2, features), BF16),
        ((16, 1, 128), jnp.int32),
        ((16, 1, 128), jnp.int32),
        None,
        ((rows, 128), F32),
        ((2, 16, CAP, SIDE), BF16),
        ((2, 16, CAP, SIDE), BF16),
        ((rows, features), F32),
        ((rows, 16 * CAP), BF16),
        ((2, rows, SIDE), BF16),
        ((2, 4, rows, SIDE), BF16),
        ((2, SIDE, channels), F32),
        ((2, channels, SIDE), F32),
        ((2, core, SIDE), BF16),
        ((2, core, SIDE), BF16),
        ((2, core, SIDE), F32),
        ((2, 4, line, SIDE), BF16),
        ((2, 4, line, SIDE), BF16),
        ((2, line, SIDE), F32),
        ((2, 8, wide, SIDE), F32),
        ((2, 8, wide, SIDE), BF16),
        ((2, 8, wide, SIDE), BF16),
        ((2, 2, 4, 8, wide, SIDE), BF16),
        ((2, core, SIDE), F32),
        ((2, 2, core, SIDE), BF16),
    ]
    split = shapes.index(None)
    counts = [1, 1, 1, 2, 2, 2, 1, 3, 2, 12, 2, 2, 2, 2, 2, 2, 2, 14, 2, 6, 2, 2]
    encoded = pl.pallas_call(
        whole_kernel,
        out_shape=jax.ShapeDtypeStruct((channels, features), BF16),
        in_specs=[anywhere] * 8,
        out_specs=anywhere,
        scratch_shapes=[pltpu.VMEM(*shape) for shape in shapes[:split]]
        + [pltpu.SMEM((16, 1, 128), jnp.int32), pltpu.SMEM((2, 1, 128), jnp.int32)]
        + [pltpu.SMEM((1, TILE), jnp.int32)] * 8
        + [pltpu.VMEM(*shape) for shape in shapes[split + 1 :]]
        + [dma((4,)), dma(()), dma((8,)), dma(()), dma(()), dma((6,)), dma((4,))]
        + [dma((n,)) for n in counts],
        compiler_params=pltpu.CompilerParams(collective_id=0, has_side_effects=True),
        name="whole",
    )(
        spectra,
        enc_weight,
        pix_tile.reshape(16, 128),
        pix_local.reshape(16, 128),
        foot_weight.reshape(16, 128),
        cotangent,
        adjoint,
        mixing,
    )
    return encoded.astype(F32)


def solution(mesh):
    finer = Mesh(
        mesh.devices.reshape(mesh.shape["obs"], 8, 2, mesh.shape["chan"]),
        ("obs", "pix_0", "pix_1", "chan"),
    )
    placed = (
        P(OBS_PIX, "chan"),
        P("chan", None),
        P(OBS_PIX, None),
        P(OBS_PIX),
        P(OBS_PIX),
        P(PIX, None),
        P(None, PIX),
        P(),
    )
    return jax.shard_map(
        shards, mesh=finer, in_specs=placed, out_specs=P("chan", None), check_vma=False
    )
```

```python
import jax
import jax.numpy as jnp
from jax import lax
from jax.experimental import pallas as pl
from jax.experimental.pallas import tpu as pltpu
from jax.sharding import Mesh
from jax.sharding import PartitionSpec as P

TILE = 4096
CAP = 64
SIDE = 128
STEPS = (4, 3, 5, 2, 6, 1, 7, 0)
PIX = ("pix_0", "pix_1")
OBS_PIX = ("obs", "pix_0", "pix_1")
AXES = ("obs", "pix_0", "pix_1", "chan")
BF16 = jnp.bfloat16
F32 = jnp.float32


def send(source, target, send_sem, recv_sem, where):
    return pltpu.make_async_remote_copy(
        src_ref=source,
        dst_ref=target,
        send_sem=send_sem,
        recv_sem=recv_sem,
        device_id=where,
        device_id_type=pl.DeviceIdType.MESH,
    )


def greet():
    barrier = pltpu.get_barrier_semaphore()
    x, z, c, y = (lax.axis_index(name) for name in AXES)
    peers = [{"obs": lax.rem(x + d, 4)} for d in range(1, 4)]
    peers += [{"chan": lax.rem(y + d, 4)} for d in range(1, 4)]
    for d in range(8):
        for e in range(2):
            if d or e:
                peers.append({"pix_0": lax.rem(z + d, 8), "pix_1": lax.rem(c + e, 2)})
    for peer in peers:
        pl.semaphore_signal(
            barrier, inc=1, device_id=peer, device_id_type=pl.DeviceIdType.MESH
        )
    return barrier, len(peers)


def one_hot(condition):
    return jnp.where(condition, 1.0, 0.0).astype(BF16)


def iota(shape, dim):
    return lax.broadcasted_iota(jnp.int32, shape, dim)


def own_rows(ref, y):
    return jnp.concatenate([ref[pl.ds(4 * y + j, 1), :] for j in range(4)], axis=1)


def ask(tile, local, weight, y, asked, columns):
    tiles, locals_, weights = own_rows(tile, y), own_rows(local, y), own_rows(weight, y)
    rows = tiles.shape[1]
    named = jnp.broadcast_to(tiles, (16, rows)) == iota((16, rows), 0)
    earlier = one_hot(iota((rows, rows), 0) < iota((rows, rows), 1))
    counts = jnp.dot(one_hot(named), earlier, preferred_element_type=F32)
    rank = jnp.sum(jnp.where(named, counts, 0.0), axis=0, keepdims=True)
    placed = one_hot(jnp.broadcast_to(rank, (128, rows)) == iota((128, rows), 0).astype(F32))
    high = lax.shift_right_logical(locals_, 6)
    low = locals_ - high * 64
    wanted = jnp.zeros((16, 128), F32)
    for digit, scale in ((high, 64.0), (low, 1.0)):
        held = jnp.where(named, jnp.broadcast_to(digit.astype(F32), (16, rows)), 0.0).astype(BF16)
        wanted += scale * lax.dot_general(
            held, placed, (((1,), (1,)), ((), ())), preferred_element_type=F32
        )
    for t in range(16):
        asked[t] = jnp.clip(wanted[t : t + 1, :].astype(jnp.int32), 0, TILE - 1)
    slot = tiles.astype(F32) * CAP + rank
    both = jnp.where(iota((128, rows), 0) == 0, jnp.broadcast_to(slot, (128, rows)),
                     jnp.broadcast_to(weights, (128, rows)))
    for j in range(rows // 128):
        block = pl.ds(j * 128, 128)
        columns[block, :] = jnp.transpose(both[:, j * 128 : (j + 1) * 128])


def widen(cot, rows_of, first, count):
    for h in range(2):
        half = cot[pl.ds(first, count), h * SIDE : (h + 1) * SIDE].astype(F32)
        rows_of[pl.ds(2 * first + h, count, stride=2), :] = half


def whole_kernel(spec_hbm, weight_hbm, tile_hbm, local_hbm, foot_hbm, cot_hbm, adjoint_hbm,
                 mixing_hbm, out, weight, tile, local, foot, adjoint, mixing, spec, cot, rows_of, mixed, near_rows, formed, parts, parts_in, relay, asked, asked_in,
                 wanted, chip_wanted, near_wanted, *rest):
    lists, rest = rest[:8], rest[8:]
    (columns, answers, answers_in, slope, chosen, part, shards, total, turned, cs, cr, mine, xs, xr,
                 xsum, zf, zs, zr, pieces, result, ordered, load_sems, cot_sem, list_sems, want_sem,
     chip_sem, near_sems, in_sems, out_sems,
     halo_s, halo_r, ask_s, ask_r, ans_s, ans_r, rs, rr, gs, gr, core_s, core_r, xs_s, xs_r, zs_s,
     zs_r, pz_s, pz_r, px_s, px_r, pc_s, pc_r) = rest
    x, z, c, y = (lax.axis_index(name) for name in AXES)
    o = 1 - c
    me = z * 2 + c
    rows = part.shape[1]
    right, left, far = lax.rem(y + 1, 4), lax.rem(y + 3, 4), lax.rem(y + 2, 4)
    to_right, to_left = {"chan": right}, {"chan": left}
    lo, hi = pl.ds(0, rows // 2), pl.ds(rows // 2, rows // 2)
    near = (1, 3, 2)
    ring = (1, 7, 2, 6, 3, 5, 4)
    sibling = {"pix_1": o}

    def go(*args):
        send(*args).start()

    def landed(ref, sem):
        send(ref, ref, sem, sem, sibling).wait_recv()

    def gone(ref, sem):
        send(ref, ref, sem, sem, sibling).wait_send()

    barrier, count = greet()
    operands = ((adjoint_hbm, adjoint), (tile_hbm, tile), (local_hbm, local), (foot_hbm, foot),
                (mixing_hbm, mixing), (weight_hbm, weight))
    loads = [pltpu.make_async_copy(a, b, in_sems.at[i]) for i, (a, b) in enumerate(operands)]
    for copy in loads[:5]:
        copy.start()
    cot_copy = pltpu.make_async_copy(cot_hbm, cot.at[pl.ds(128, TILE)], cot_sem)
    cot_copy.start()
    loads[5].start()
    loads[0].wait()
    inside = jnp.clip(adjoint[...] - (me * TILE - SIDE), 0, TILE + 2 * SIDE - 1)
    near_rows[...] = inside * 2
    list_copies = []
    for k in range(8):
        copy = pltpu.make_async_copy(near_rows.at[pl.ds(k, 1)], lists[k], list_sems.at[k])
        copy.start()
        list_copies.append(copy)
    for copy in loads[1:5]:
        copy.wait()
    ask(tile, local, foot, y, asked, columns)
    asked_in[me] = asked[me]
    owners = (far, right, left, y)
    spec_copies = []
    for step, owner in enumerate(owners):
        block = pl.ds(pl.multiple_of(owner * rows, rows), rows)
        copy = pltpu.make_async_copy(spec_hbm.at[block], spec.at[block], load_sems.at[step])
        copy.start()
        spec_copies.append(copy)
    for k in range(8):
        for h in range(2):
            mixed[pl.ds(2 * k + h, 1), :] = mixing[pl.ds(k, 1), h * SIDE : (h + 1) * SIDE]

    order = [(d, e) for d in STEPS for e in (1, 0)]

    def pair(k, ahead):
        d, e = order[k]
        return lax.rem(z + (d if ahead else 8 - d), 8), lax.rem(c + e, 2)

    after = {"pix_0": lax.rem(z + c, 8), "pix_1": o}
    before = {"pix_0": lax.rem(z + 7 + c, 8), "pix_1": o}
    pl.semaphore_wait(barrier, count)
    for k in range(15):
        zz, cc = pair(k, True)
        go(asked.at[zz * 2 + cc], asked_in.at[me], ask_s.at[0], ask_r.at[(k >= 10) + (k == 14)],
           {"pix_0": zz, "pix_1": cc})
    ends = cot.at[pl.ds(0, SIDE)], cot.at[pl.ds(TILE + SIDE, SIDE)]
    go(cot_hbm.at[pl.ds(0, SIDE)], ends[1], halo_s.at[0], halo_r.at[0], before)
    go(cot_hbm.at[pl.ds(TILE - SIDE, SIDE)], ends[0], halo_s.at[0], halo_r.at[0], after)

    cot_copy.wait()

    def widen_step(i, carry):
        widen(cot, rows_of, pl.multiple_of(SIDE + i * 256, SIDE), 256)
        return carry

    lax.fori_loop(0, TILE // 256, widen_step, 0)

    loads[5].wait()

    def encode(step):
        owner = owners[step]
        spec_copies[step].wait()
        block = spec[pl.ds(pl.multiple_of(owner * rows, rows), rows), :]
        parts[owner] = jnp.dot(block, weight[...], preferred_element_type=F32).astype(BF16)

    encode(0)
    go(parts.at[far, lo], relay.at[0], rs.at[0], rr.at[0], to_right)
    go(parts.at[far, hi], relay.at[1], rs.at[0], rr.at[1], to_left)
    encode(1)
    go(parts.at[right], parts_in.at[y], rs.at[0], rr.at[2], to_right)
    encode(2)
    go(parts.at[left], parts_in.at[y], rs.at[0], rr.at[2], to_left)
    landed(cot.at[pl.ds(0, 2 * SIDE)], halo_r.at[0])
    widen(cot, rows_of, 0, SIDE)
    widen(cot, rows_of, TILE + SIDE, SIDE)
    for copy in list_copies:
        copy.wait()

    def serve(k, source, slot):
        mix = [mixed[pl.ds(2 * n, 2), :] for n in range(8)]
        unroll = 32

        def some(i, carry):
            for u in range(unroll):
                at = i * unroll + u
                pixel = source[slot, 0, at]
                row = rows_of[pl.ds(pixel * 2 + 2 * SIDE, 2), :]
                for n in range(8):
                    row = row + rows_of[pl.ds(lists[n][0, pixel], 2), :] * mix[n]
                formed[pl.ds(k % 2 * 2 * CAP + 2 * at, 2), :] = row
            return carry

        lax.fori_loop(0, CAP // unroll, some, 0)
        for h in range(2):
            half = formed[pl.ds(k % 2 * 2 * CAP + h, CAP, stride=2), :]
            answers[h, k] = half.astype(BF16)

    def reply(h, k):
        zz, cc = pair(k, False)
        go(answers.at[h, k], answers_in.at[h, me], ans_s.at[h], ans_r.at[h],
           {"pix_0": zz, "pix_1": cc})

    landed(asked_in.at[0], ask_r.at[2])
    chip_copy = pltpu.make_async_copy(asked_in.at[pl.ds(2 * z, 2)], chip_wanted, chip_sem)
    chip_copy.start()
    chip_copy.wait()
    serve(15, chip_wanted, c)
    landed(asked_in.at[pl.ds(0, 4)], ask_r.at[1])
    near_copies = []
    for i, d in enumerate((1, 7)):
        rows_in = asked_in.at[pl.ds(2 * lax.rem(z + 8 - d, 8), 2)]
        target = near_wanted.at[pl.ds(2 * i, 2)]
        near_copies.append(pltpu.make_async_copy(rows_in, target, near_sems.at[i]))
        near_copies[i].start()
    serve(14, chip_wanted, o)
    reply(0, 14)
    for h in range(2):
        answers_in[h, me] = answers[h, 15]
    for copy in near_copies:
        copy.wait()
    served = [14]
    lag = 15

    def serve_and_reply(k, source, slot):
        serve(k, source, slot)
        reply(0, k)
        served.append(k)
        if len(served) > lag:
            reply(1, served[len(served) - lag - 1])

    for k in (10, 11, 12):
        d, e = order[k]
        serve_and_reply(k, near_wanted, (0 if d == 1 else 2) + lax.rem(c + e, 2))
        if k == 11:
            landed(relay.at[0], rr.at[0])
            go(relay.at[0], parts_in.at[left, lo], rs.at[0], rr.at[2], to_right)
            landed(relay.at[1], rr.at[1])
            go(relay.at[1], parts_in.at[right, hi], rs.at[0], rr.at[2], to_left)
    landed(asked_in.at[pl.ds(0, 10)], ask_r.at[0])
    want_copy = pltpu.make_async_copy(asked_in, wanted, want_sem)
    want_copy.start()
    serve_and_reply(13, near_wanted, 2 + lax.rem(c + order[13][1], 2))
    want_copy.wait()
    for k in range(10):
        zz, cc = pair(k, False)
        serve_and_reply(k, wanted, zz * 2 + cc)
    for k in served[-lag:]:
        reply(1, k)
    encode(3)

    slots = 16 * CAP
    chosen[...] = one_hot(
        jnp.broadcast_to(columns[:, 0:1], (rows, slots)) == iota((rows, slots), 1).astype(F32)
    )
    landed(parts_in.at[pl.ds(0, 3)], rr.at[2])
    pre = parts[y].astype(F32)
    for origin in (left, right, far):
        pre = pre + parts_in[origin].astype(F32)
    sigma = 1.0 / (1.0 + jnp.exp(-pre))
    slope[...] = columns[:, 1:2] * (sigma * (1.0 + pre * (1.0 - sigma)))

    def fetch(h):
        landed(answers_in.at[h, pl.ds(0, 15)], ans_r.at[h])
        rows_in = answers_in[h].reshape(slots, SIDE)
        fetched = jnp.dot(chosen[...], rows_in, preferred_element_type=F32)
        part[h] = (slope[:, h * SIDE : (h + 1) * SIDE] * fetched).astype(BF16)

    def multiply(h, gradient, owner, fresh=False):
        flat = jnp.transpose(gradient.astype(F32)).astype(BF16)
        width = spec.shape[1] // 3
        for n in range(3):
            cols = pl.ds(n * width, width)
            block = spec[pl.ds(pl.multiple_of(owner * rows, rows), rows), cols]
            product = jnp.dot(flat, block, preferred_element_type=F32)
            if fresh:
                total[h, :, cols] = product
            else:
                total[h, :, cols] += product

    def gather_start(h):
        i = h * 6
        mine_, store = part.at[h], shards.at[h]
        go(mine_.at[lo], store.at[y, lo], gs.at[h], gr.at[i], to_right)
        go(mine_.at[hi], store.at[y, hi], gs.at[h], gr.at[i + 1], to_left)
        multiply(h, part[h], y, True)
        go(mine_.at[hi], store.at[y, hi], gs.at[h], gr.at[i + 2], to_right)
        go(mine_.at[lo], store.at[y, lo], gs.at[h], gr.at[i + 3], to_left)

    def gather_relay(h):
        i = h * 6
        store = shards.at[h]
        landed(store.at[left, lo], gr.at[i])
        go(store.at[left, lo], store.at[left, lo], gs.at[h], gr.at[i + 4], to_right)
        landed(store.at[right, hi], gr.at[i + 1])
        go(store.at[right, hi], store.at[right, hi], gs.at[h], gr.at[i + 5], to_left)

    def gather_near(h):
        i = h * 6
        store = shards.at[h]
        landed(store.at[left, hi], gr.at[i + 2])
        multiply(h, shards[h, left], left)
        landed(store.at[right, lo], gr.at[i + 3])
        multiply(h, shards[h, right], right)

    core_lines, line, wide = mine.shape[1], xs.shape[2], zs.shape[2]

    def gather_far(h):
        i = h * 6
        store = shards.at[h]
        landed(store.at[far, lo], gr.at[i + 4])
        landed(store.at[far, hi], gr.at[i + 5])
        multiply(h, shards[h, far], far)
        for j in range(total.shape[2] // SIDE):
            block = pl.ds(j * SIDE, SIDE)
            turned[h, block, :] = jnp.transpose(total[h, :, block])
        theirs = pl.ds(pl.multiple_of(o * core_lines, 8), core_lines)
        cs[h] = turned[h, theirs, :].astype(BF16)
        go(cs.at[h], cr.at[h], core_s.at[h], core_r.at[h], {"pix_1": o})

    def core_sum(h):
        landed(cr.at[h], core_r.at[h])
        ours = pl.ds(pl.multiple_of(c * core_lines, 8), core_lines)
        mine[h] = turned[h, ours, :] + cr[h].astype(F32)
        for j in range(4):
            xs[h, j] = mine[h, pl.ds(j * line, line), :].astype(BF16)
        for d in near:
            peer = lax.rem(x + d, 4)
            go(xs.at[h, peer], xr.at[h, x], xs_s.at[h], xs_r.at[h], {"obs": peer})

    def x_sum(h):
        summed = mine[h, pl.ds(pl.multiple_of(x * line, 8), line), :]
        landed(xr.at[h, pl.ds(0, 3)], xs_r.at[h])
        for d in near:
            summed = summed + xr[h, lax.rem(x + 4 - d, 4)].astype(F32)
        xsum[h] = summed
        for j in range(8):
            zf[h, j] = xsum[h, pl.ds(j * wide, wide), :]
            zs[h, j] = zf[h, j].astype(BF16)
        for d in ring:
            peer = lax.rem(z + d, 8)
            go(zs.at[h, peer], zr.at[h, z], zs_s.at[h], zs_r.at[h], {"pix_0": peer})

    def z_sum(h):
        own = zf[h, z]
        landed(zr.at[h, pl.ds(0, 7)], zs_r.at[h])
        for d in ring:
            own = own + zr[h, lax.rem(z + 8 - d, 8)].astype(F32)
        pieces[h, c, x, z] = own.astype(BF16)
        piece = pieces.at[h, c, x, z]
        for d in ring:
            at = h * 7 + d - 1
            go(piece, piece, pz_s.at[h], pz_r.at[at], {"pix_0": lax.rem(z + d, 8)})

    def z_gather(h):
        for d in (0,) + ring:
            origin = lax.rem(z + 8 - d, 8)
            piece = pieces.at[h, c, x, origin]
            if d:
                landed(piece, pz_r.at[h * 7 + d - 1])
            for e in near:
                at = h * 3 + e - 1
                go(piece, piece, px_s.at[h], px_r.at[at], {"obs": lax.rem(x + e, 4)})
        group = pieces.at[h, c, x]
        go(group, group, pc_s.at[h], pc_r.at[h], {"pix_1": o})

    def assemble(h, core):
        for xx in range(4):
            for zz in range(8):
                row = xx * line + zz * wide
                result[core, pl.ds(row, wide), :] = pieces[h, core, xx, zz].astype(F32)
        ordered[h, core] = result[core].astype(BF16)
        target = out.at[pl.ds(pl.multiple_of(core * core_lines, 8), core_lines),
                        pl.ds(h * SIDE, SIDE)]
        copy = pltpu.make_async_copy(ordered.at[h, core], target, out_sems.at[len(results)])
        copy.start()
        results.append(copy)

    results = []

    def x_gather(h):
        for e in near:
            column = lax.rem(x + 4 - e, 4)
            group = pieces.at[h, c, column]
            landed(group, px_r.at[h * 3 + e - 1])
            go(group, group, pc_s.at[h], pc_r.at[h], {"pix_1": o})
        assemble(h, c)

    def core_gather(h):
        landed(pieces.at[h, o], pc_r.at[h])
        assemble(h, o)

    fetch(0)
    gather_start(0)
    gather_relay(0)
    gather_near(0)
    fetch(1)
    gather_start(1)
    gather_far(0)
    gather_relay(1)
    core_sum(0)
    gather_near(1)
    gather_far(1)
    core_sum(1)
    x_sum(0)
    gone(asked.at[pl.ds(0, 15)], ask_s.at[0])
    gone(cot.at[pl.ds(0, 2 * SIDE)], halo_s.at[0])
    gone(parts, rs.at[0])
    for h in range(2):
        gone(answers.at[h, pl.ds(0, 15)], ans_s.at[h])
        gone(shards.at[h, pl.ds(0, 3)], gs.at[h])
    x_sum(1)
    z_sum(0)
    for h in range(2):
        gone(cs.at[h], core_s.at[h])
        gone(xs.at[h, pl.ds(0, 3)], xs_s.at[h])
    z_sum(1)
    z_gather(0)
    for h in range(2):
        gone(zs.at[h, pl.ds(0, 7)], zs_s.at[h])
    x_gather(0)
    z_gather(1)
    core_gather(0)
    for h in range(2):
        gone(pieces.at[h, 0, 0, pl.ds(0, 7)], pz_s.at[h])
    gone(pieces.at[0, 0, pl.ds(0, 3)], px_s.at[0])
    x_gather(1)
    core_gather(1)
    gone(pieces.at[1, 0, pl.ds(0, 3)], px_s.at[1])
    for h in range(2):
        gone(pieces.at[h, 0], pc_s.at[h])
    for copy in results:
        copy.wait()


def widen_kernel(narrow, wide, held, filled, in_sems, out_sems):
    lines = held.shape[1]
    arriving, leaving = [], []
    for i in range(held.shape[0]):
        rows = pl.ds(i * lines, lines)
        arriving.append(pltpu.make_async_copy(narrow.at[rows], held.at[i], in_sems.at[i]))
        leaving.append(pltpu.make_async_copy(filled.at[i], wide.at[rows], out_sems.at[i]))
        arriving[i].start()
    for i in range(held.shape[0]):
        arriving[i].wait()
        filled[i] = held[i].astype(F32)
        leaving[i].start()
    for copy in leaving:
        copy.wait()


def widened(narrow):
    rows, columns = narrow.shape
    count = 4
    chunk = (count, rows // count, columns)
    anywhere = pl.BlockSpec(memory_space=pl.ANY)
    return pl.pallas_call(
        widen_kernel,
        out_shape=jax.ShapeDtypeStruct(narrow.shape, F32),
        in_specs=[anywhere],
        out_specs=anywhere,
        scratch_shapes=[
            pltpu.VMEM(chunk, BF16),
            pltpu.VMEM(chunk, F32),
            pltpu.SemaphoreType.DMA((count,)),
            pltpu.SemaphoreType.DMA((count,)),
        ],
        name="widen",
    )(narrow)


def shards(spectra, enc_weight, pix_tile, pix_local, foot_weight, cotangent, adjoint, mixing):
    rows, features = spectra.shape[0] // 4, cotangent.shape[1]
    channels = spectra.shape[1]
    dma = pltpu.SemaphoreType.DMA
    anywhere = pl.BlockSpec(memory_space=pl.ANY)
    core, line, wide = channels // 2, channels // 8, channels // 64
    shapes = [
        (enc_weight.shape, BF16),
        ((16, 128), jnp.int32),
        ((16, 128), jnp.int32),
        ((16, 128), F32),
        (adjoint.shape, jnp.int32),
        (mixing.shape, F32),
        (spectra.shape, BF16),
        ((TILE + 256, features), BF16),
        ((2 * TILE + 520, SIDE), F32),
        ((16, SIDE), F32),
        ((8, TILE), jnp.int32),
        ((4 * CAP + 8, SIDE), F32),
        ((4, rows, features), BF16),
        ((4, rows, features), BF16),
        ((2, rows // 2, features), BF16),
        ((16, 1, 128), jnp.int32),
        ((16, 1, 128), jnp.int32),
        None,
        ((rows, 128), F32),
        ((2, 16, CAP, SIDE), BF16),
        ((2, 16, CAP, SIDE), BF16),
        ((rows, features), F32),
        ((rows, 16 * CAP), BF16),
        ((2, rows, SIDE), BF16),
        ((2, 4, rows, SIDE), BF16),
        ((2, SIDE, channels), F32),
        ((2, channels, SIDE), F32),
        ((2, core, SIDE), BF16),
        ((2, core, SIDE), BF16),
        ((2, core, SIDE), F32),
        ((2, 4, line, SIDE), BF16),
        ((2, 4, line, SIDE), BF16),
        ((2, line, SIDE), F32),
        ((2, 8, wide, SIDE), F32),
        ((2, 8, wide, SIDE), BF16),
        ((2, 8, wide, SIDE), BF16),
        ((2, 2, 4, 8, wide, SIDE), BF16),
        ((2, core, SIDE), F32),
        ((2, 2, core, SIDE), BF16),
    ]
    split = shapes.index(None)
    counts = [1, 1, 1, 3, 2, 2, 1, 3, 2, 12, 2, 2, 2, 2, 2, 2, 2, 14, 2, 6, 2, 2]
    encoded = pl.pallas_call(
        whole_kernel,
        out_shape=jax.ShapeDtypeStruct((channels, features), BF16),
        in_specs=[anywhere] * 8,
        out_specs=anywhere,
        scratch_shapes=[pltpu.VMEM(*shape) for shape in shapes[:split]]
        + [pltpu.SMEM((16, 1, 128), jnp.int32), pltpu.SMEM((2, 1, 128), jnp.int32)]
        + [pltpu.SMEM((4, 1, 128), jnp.int32)]
        + [pltpu.SMEM((1, TILE), jnp.int32)] * 8
        + [pltpu.VMEM(*shape) for shape in shapes[split + 1 :]]
        + [dma((4,)), dma(()), dma((8,)), dma(()), dma(()), dma((2,)), dma((6,)), dma((4,))]
        + [dma((n,)) for n in counts],
        compiler_params=pltpu.CompilerParams(collective_id=0, has_side_effects=True),
        name="whole",
    )(
        spectra,
        enc_weight,
        pix_tile.reshape(16, 128),
        pix_local.reshape(16, 128),
        foot_weight.reshape(16, 128),
        cotangent,
        adjoint,
        mixing,
    )
    return widened(encoded)


def solution(mesh):
    finer = Mesh(
        mesh.devices.reshape(mesh.shape["obs"], 8, 2, mesh.shape["chan"]),
        ("obs", "pix_0", "pix_1", "chan"),
    )
    placed = (
        P(OBS_PIX, "chan"),
        P("chan", None),
        P(OBS_PIX, None),
        P(OBS_PIX),
        P(OBS_PIX),
        P(PIX, None),
        P(None, PIX),
        P(),
    )
    return jax.shard_map(
        shards, mesh=finer, in_specs=placed, out_specs=P("chan", None), check_vma=False
    )
```

```python
import jax
import jax.numpy as jnp
from jax import lax
from jax.experimental import pallas as pl
from jax.experimental.pallas import tpu as pltpu
from jax.sharding import Mesh
from jax.sharding import PartitionSpec as P

TILE = 4096
CAP = 64
SIDE = 128
STEPS = (4, 3, 5, 2, 6, 1, 7, 0)
PIX = ("pix_0", "pix_1")
OBS_PIX = ("obs", "pix_0", "pix_1")
AXES = ("obs", "pix_0", "pix_1", "chan")
BF16 = jnp.bfloat16
F32 = jnp.float32


def send(source, target, send_sem, recv_sem, where):
    return pltpu.make_async_remote_copy(
        src_ref=source,
        dst_ref=target,
        send_sem=send_sem,
        recv_sem=recv_sem,
        device_id=where,
        device_id_type=pl.DeviceIdType.MESH,
    )


def greet():
    barrier = pltpu.get_barrier_semaphore()
    x, z, c, y = (lax.axis_index(name) for name in AXES)
    peers = [{"obs": lax.rem(x + d, 4)} for d in range(1, 4)]
    peers += [{"chan": lax.rem(y + d, 4)} for d in range(1, 4)]
    for d in range(8):
        for e in range(2):
            if d or e:
                peers.append({"pix_0": lax.rem(z + d, 8), "pix_1": lax.rem(c + e, 2)})
    for peer in peers:
        pl.semaphore_signal(
            barrier, inc=1, device_id=peer, device_id_type=pl.DeviceIdType.MESH
        )
    return barrier, len(peers)


def one_hot(condition):
    return jnp.where(condition, 1.0, 0.0).astype(BF16)


def iota(shape, dim):
    return lax.broadcasted_iota(jnp.int32, shape, dim)


def own_rows(ref, y):
    return jnp.concatenate([ref[pl.ds(4 * y + j, 1), :] for j in range(4)], axis=1)


def ask(tile, local, weight, y, asked, columns):
    tiles, locals_, weights = own_rows(tile, y), own_rows(local, y), own_rows(weight, y)
    rows = tiles.shape[1]
    named = jnp.broadcast_to(tiles, (16, rows)) == iota((16, rows), 0)
    earlier = one_hot(iota((rows, rows), 0) < iota((rows, rows), 1))
    counts = jnp.dot(one_hot(named), earlier, preferred_element_type=F32)
    rank = jnp.sum(jnp.where(named, counts, 0.0), axis=0, keepdims=True)
    placed = one_hot(jnp.broadcast_to(rank, (128, rows)) == iota((128, rows), 0).astype(F32))
    high = lax.shift_right_logical(locals_, 6)
    low = locals_ - high * 64
    wanted = jnp.zeros((16, 128), F32)
    for digit, scale in ((high, 64.0), (low, 1.0)):
        held = jnp.where(named, jnp.broadcast_to(digit.astype(F32), (16, rows)), 0.0).astype(BF16)
        wanted += scale * lax.dot_general(
            held, placed, (((1,), (1,)), ((), ())), preferred_element_type=F32
        )
    for t in range(16):
        asked[t] = jnp.clip(wanted[t : t + 1, :].astype(jnp.int32), 0, TILE - 1)
    slot = tiles.astype(F32) * CAP + rank
    both = jnp.where(iota((128, rows), 0) == 0, jnp.broadcast_to(slot, (128, rows)),
                     jnp.broadcast_to(weights, (128, rows)))
    for j in range(rows // 128):
        block = pl.ds(j * 128, 128)
        columns[block, :] = jnp.transpose(both[:, j * 128 : (j + 1) * 128])


def widen(cot, rows_of, first, count):
    for h in range(2):
        half = cot[pl.ds(first, count), h * SIDE : (h + 1) * SIDE].astype(F32)
        rows_of[pl.ds(2 * first + h, count, stride=2), :] = half


def whole_kernel(spec_hbm, weight_hbm, tile_hbm, local_hbm, foot_hbm, cot_hbm, adjoint_hbm,
                 mixing_hbm, out, weight, tile, local, foot, adjoint, mixing, spec, cot, rows_of, mixed, near_rows, formed, parts, parts_in, relay, asked, asked_in,
                 wanted, chip_wanted, near_wanted, *rest):
    lists, rest = rest[:8], rest[8:]
    (columns, answers, answers_in, slope, chosen, part, shards, total, turned, cs, cr, mine, xs, xr,
                 xsum, zf, zs, zr, pieces, result, ordered, load_sems, cot_sem, list_sems, want_sem,
     chip_sem, near_sems, in_sems, out_sems,
     halo_s, halo_r, ask_s, ask_r, ans_s, ans_r, rs, rr, gs, gr, core_s, core_r, xs_s, xs_r, zs_s,
     zs_r, pz_s, pz_r, px_s, px_r, pc_s, pc_r) = rest
    x, z, c, y = (lax.axis_index(name) for name in AXES)
    o = 1 - c
    me = z * 2 + c
    rows = part.shape[1]
    right, left, far = lax.rem(y + 1, 4), lax.rem(y + 3, 4), lax.rem(y + 2, 4)
    to_right, to_left = {"chan": right}, {"chan": left}
    lo, hi = pl.ds(0, rows // 2), pl.ds(rows // 2, rows // 2)
    near = (1, 3, 2)
    ring = (1, 7, 2, 6, 3, 5, 4)
    sibling = {"pix_1": o}

    def go(*args):
        send(*args).start()

    def landed(ref, sem):
        send(ref, ref, sem, sem, sibling).wait_recv()

    def gone(ref, sem):
        send(ref, ref, sem, sem, sibling).wait_send()

    barrier, count = greet()
    operands = ((adjoint_hbm, adjoint), (tile_hbm, tile), (local_hbm, local), (foot_hbm, foot),
                (mixing_hbm, mixing), (weight_hbm, weight))
    loads = [pltpu.make_async_copy(a, b, in_sems.at[i]) for i, (a, b) in enumerate(operands)]
    for copy in loads[:5]:
        copy.start()
    cot_copy = pltpu.make_async_copy(cot_hbm, cot.at[pl.ds(128, TILE)], cot_sem)
    cot_copy.start()
    loads[5].start()
    loads[0].wait()
    inside = jnp.clip(adjoint[...] - (me * TILE - SIDE), 0, TILE + 2 * SIDE - 1)
    near_rows[...] = inside * 2
    list_copies = []
    for k in range(8):
        copy = pltpu.make_async_copy(near_rows.at[pl.ds(k, 1)], lists[k], list_sems.at[k])
        copy.start()
        list_copies.append(copy)
    for copy in loads[1:5]:
        copy.wait()
    ask(tile, local, foot, y, asked, columns)
    asked_in[me] = asked[me]
    owners = (far, right, left, y)
    spec_copies = []
    for step, owner in enumerate(owners):
        block = pl.ds(pl.multiple_of(owner * rows, rows), rows)
        copy = pltpu.make_async_copy(spec_hbm.at[block], spec.at[block], load_sems.at[step])
        copy.start()
        spec_copies.append(copy)
    for k in range(8):
        for h in range(2):
            mixed[pl.ds(2 * k + h, 1), :] = mixing[pl.ds(k, 1), h * SIDE : (h + 1) * SIDE]

    order = [(d, e) for d in STEPS for e in (1, 0)]

    def pair(k, ahead):
        d, e = order[k]
        return lax.rem(z + (d if ahead else 8 - d), 8), lax.rem(c + e, 2)

    after = {"pix_0": lax.rem(z + c, 8), "pix_1": o}
    before = {"pix_0": lax.rem(z + 7 + c, 8), "pix_1": o}
    pl.semaphore_wait(barrier, count)
    for k in range(15):
        zz, cc = pair(k, True)
        go(asked.at[zz * 2 + cc], asked_in.at[me], ask_s.at[0], ask_r.at[(k >= 10) + (k == 14)],
           {"pix_0": zz, "pix_1": cc})
    ends = cot.at[pl.ds(0, SIDE)], cot.at[pl.ds(TILE + SIDE, SIDE)]
    go(cot_hbm.at[pl.ds(0, SIDE)], ends[1], halo_s.at[0], halo_r.at[0], before)
    go(cot_hbm.at[pl.ds(TILE - SIDE, SIDE)], ends[0], halo_s.at[0], halo_r.at[0], after)

    cot_copy.wait()

    def widen_step(i, carry):
        widen(cot, rows_of, pl.multiple_of(SIDE + i * 256, SIDE), 256)
        return carry

    lax.fori_loop(0, TILE // 256, widen_step, 0)

    loads[5].wait()

    def encode(step):
        owner = owners[step]
        spec_copies[step].wait()
        block = spec[pl.ds(pl.multiple_of(owner * rows, rows), rows), :]
        parts[owner] = jnp.dot(block, weight[...], preferred_element_type=F32).astype(BF16)

    encode(0)
    go(parts.at[far, lo], relay.at[0], rs.at[0], rr.at[0], to_right)
    go(parts.at[far, hi], relay.at[1], rs.at[0], rr.at[1], to_left)
    encode(1)
    go(parts.at[right], parts_in.at[y], rs.at[0], rr.at[2], to_right)
    encode(2)
    go(parts.at[left], parts_in.at[y], rs.at[0], rr.at[2], to_left)
    landed(cot.at[pl.ds(0, 2 * SIDE)], halo_r.at[0])
    widen(cot, rows_of, 0, SIDE)
    widen(cot, rows_of, TILE + SIDE, SIDE)
    for copy in list_copies:
        copy.wait()

    def serve(k, source, slot):
        mix = [mixed[pl.ds(2 * n, 2), :] for n in range(8)]
        unroll = 32

        def some(i, carry):
            for u in range(unroll):
                at = i * unroll + u
                pixel = source[slot, 0, at]
                row = rows_of[pl.ds(pixel * 2 + 2 * SIDE, 2), :]
                for n in range(8):
                    row = row + rows_of[pl.ds(lists[n][0, pixel], 2), :] * mix[n]
                formed[pl.ds(k % 2 * 2 * CAP + 2 * at, 2), :] = row
            return carry

        lax.fori_loop(0, CAP // unroll, some, 0)
        for h in range(2):
            half = formed[pl.ds(k % 2 * 2 * CAP + h, CAP, stride=2), :]
            answers[h, k] = half.astype(BF16)

    def reply(h, k):
        zz, cc = pair(k, False)
        go(answers.at[h, k], answers_in.at[h, me], ans_s.at[h], ans_r.at[h],
           {"pix_0": zz, "pix_1": cc})

    landed(asked_in.at[0], ask_r.at[2])
    chip_copy = pltpu.make_async_copy(asked_in.at[pl.ds(2 * z, 2)], chip_wanted, chip_sem)
    chip_copy.start()
    chip_copy.wait()
    serve(15, chip_wanted, c)
    landed(asked_in.at[pl.ds(0, 4)], ask_r.at[1])
    near_copies = []
    for i, d in enumerate((1, 7)):
        rows_in = asked_in.at[pl.ds(2 * lax.rem(z + 8 - d, 8), 2)]
        target = near_wanted.at[pl.ds(2 * i, 2)]
        near_copies.append(pltpu.make_async_copy(rows_in, target, near_sems.at[i]))
        near_copies[i].start()
    serve(14, chip_wanted, o)
    reply(0, 14)
    for h in range(2):
        answers_in[h, me] = answers[h, 15]
    for copy in near_copies:
        copy.wait()
    served = [14]
    lag = 12

    def serve_and_reply(k, source, slot):
        serve(k, source, slot)
        reply(0, k)
        served.append(k)
        if len(served) > lag:
            reply(1, served[len(served) - lag - 1])

    for k in (10, 11, 12):
        d, e = order[k]
        serve_and_reply(k, near_wanted, (0 if d == 1 else 2) + lax.rem(c + e, 2))
    landed(asked_in.at[pl.ds(0, 10)], ask_r.at[0])
    want_copy = pltpu.make_async_copy(asked_in, wanted, want_sem)
    want_copy.start()
    serve_and_reply(13, near_wanted, 2 + lax.rem(c + order[13][1], 2))
    want_copy.wait()
    for k in range(10):
        zz, cc = pair(k, False)
        serve_and_reply(k, wanted, zz * 2 + cc)
        if k == 0:
            landed(relay.at[0], rr.at[0])
            go(relay.at[0], parts_in.at[left, lo], rs.at[0], rr.at[2], to_right)
            landed(relay.at[1], rr.at[1])
            go(relay.at[1], parts_in.at[right, hi], rs.at[0], rr.at[2], to_left)
    for k in served[-lag:]:
        reply(1, k)
    encode(3)

    slots = 16 * CAP
    chosen[...] = one_hot(
        jnp.broadcast_to(columns[:, 0:1], (rows, slots)) == iota((rows, slots), 1).astype(F32)
    )
    landed(parts_in.at[pl.ds(0, 3)], rr.at[2])
    pre = parts[y].astype(F32)
    for origin in (left, right, far):
        pre = pre + parts_in[origin].astype(F32)
    sigma = 1.0 / (1.0 + jnp.exp(-pre))
    slope[...] = columns[:, 1:2] * (sigma * (1.0 + pre * (1.0 - sigma)))

    def fetch(h):
        landed(answers_in.at[h, pl.ds(0, 15)], ans_r.at[h])
        rows_in = answers_in[h].reshape(slots, SIDE)
        fetched = jnp.dot(chosen[...], rows_in, preferred_element_type=F32)
        part[h] = (slope[:, h * SIDE : (h + 1) * SIDE] * fetched).astype(BF16)

    def multiply(h, gradient, owner, fresh=False):
        flat = jnp.transpose(gradient.astype(F32)).astype(BF16)
        width = spec.shape[1] // 3
        for n in range(3):
            cols = pl.ds(n * width, width)
            block = spec[pl.ds(pl.multiple_of(owner * rows, rows), rows), cols]
            product = jnp.dot(flat, block, preferred_element_type=F32)
            if fresh:
                total[h, :, cols] = product
            else:
                total[h, :, cols] += product

    def gather_start(h):
        i = h * 6
        mine_, store = part.at[h], shards.at[h]
        go(mine_.at[lo], store.at[y, lo], gs.at[h], gr.at[i], to_right)
        go(mine_.at[hi], store.at[y, hi], gs.at[h], gr.at[i + 1], to_left)
        multiply(h, part[h], y, True)
        go(mine_.at[hi], store.at[y, hi], gs.at[h], gr.at[i + 2], to_right)
        go(mine_.at[lo], store.at[y, lo], gs.at[h], gr.at[i + 3], to_left)

    def gather_relay(h):
        i = h * 6
        store = shards.at[h]
        landed(store.at[left, lo], gr.at[i])
        go(store.at[left, lo], store.at[left, lo], gs.at[h], gr.at[i + 4], to_right)
        landed(store.at[right, hi], gr.at[i + 1])
        go(store.at[right, hi], store.at[right, hi], gs.at[h], gr.at[i + 5], to_left)

    def gather_near(h):
        i = h * 6
        store = shards.at[h]
        landed(store.at[left, hi], gr.at[i + 2])
        multiply(h, shards[h, left], left)
        landed(store.at[right, lo], gr.at[i + 3])
        multiply(h, shards[h, right], right)

    core_lines, line, wide = mine.shape[1], xs.shape[2], zs.shape[2]

    def gather_far(h):
        i = h * 6
        store = shards.at[h]
        landed(store.at[far, lo], gr.at[i + 4])
        landed(store.at[far, hi], gr.at[i + 5])
        multiply(h, shards[h, far], far)
        for j in range(total.shape[2] // SIDE):
            block = pl.ds(j * SIDE, SIDE)
            turned[h, block, :] = jnp.transpose(total[h, :, block])
        theirs = pl.ds(pl.multiple_of(o * core_lines, 8), core_lines)
        cs[h] = turned[h, theirs, :].astype(BF16)
        go(cs.at[h], cr.at[h], core_s.at[h], core_r.at[h], {"pix_1": o})

    def core_sum(h):
        landed(cr.at[h], core_r.at[h])
        ours = pl.ds(pl.multiple_of(c * core_lines, 8), core_lines)
        mine[h] = turned[h, ours, :] + cr[h].astype(F32)
        for j in range(4):
            xs[h, j] = mine[h, pl.ds(j * line, line), :].astype(BF16)
        for d in near:
            peer = lax.rem(x + d, 4)
            go(xs.at[h, peer], xr.at[h, x], xs_s.at[h], xs_r.at[h], {"obs": peer})

    def x_sum(h):
        summed = mine[h, pl.ds(pl.multiple_of(x * line, 8), line), :]
        landed(xr.at[h, pl.ds(0, 3)], xs_r.at[h])
        for d in near:
            summed = summed + xr[h, lax.rem(x + 4 - d, 4)].astype(F32)
        xsum[h] = summed
        for j in range(8):
            zf[h, j] = xsum[h, pl.ds(j * wide, wide), :]
            zs[h, j] = zf[h, j].astype(BF16)
        for d in ring:
            peer = lax.rem(z + d, 8)
            go(zs.at[h, peer], zr.at[h, z], zs_s.at[h], zs_r.at[h], {"pix_0": peer})

    def z_sum(h):
        own = zf[h, z]
        landed(zr.at[h, pl.ds(0, 7)], zs_r.at[h])
        for d in ring:
            own = own + zr[h, lax.rem(z + 8 - d, 8)].astype(F32)
        pieces[h, c, x, z] = own.astype(BF16)
        piece = pieces.at[h, c, x, z]
        for d in ring:
            at = h * 7 + d - 1
            go(piece, piece, pz_s.at[h], pz_r.at[at], {"pix_0": lax.rem(z + d, 8)})

    def z_gather(h):
        for d in (0,) + ring:
            origin = lax.rem(z + 8 - d, 8)
            piece = pieces.at[h, c, x, origin]
            if d:
                landed(piece, pz_r.at[h * 7 + d - 1])
            for e in near:
                at = h * 3 + e - 1
                go(piece, piece, px_s.at[h], px_r.at[at], {"obs": lax.rem(x + e, 4)})
        group = pieces.at[h, c, x]
        go(group, group, pc_s.at[h], pc_r.at[h], {"pix_1": o})

    def assemble(h, core):
        for xx in range(4):
            for zz in range(8):
                row = xx * line + zz * wide
                result[core, pl.ds(row, wide), :] = pieces[h, core, xx, zz].astype(F32)
        ordered[h, core] = result[core].astype(BF16)
        target = out.at[pl.ds(pl.multiple_of(core * core_lines, 8), core_lines),
                        pl.ds(h * SIDE, SIDE)]
        copy = pltpu.make_async_copy(ordered.at[h, core], target, out_sems.at[len(results)])
        copy.start()
        results.append(copy)

    results = []

    def x_gather(h):
        for e in near:
            column = lax.rem(x + 4 - e, 4)
            group = pieces.at[h, c, column]
            landed(group, px_r.at[h * 3 + e - 1])
            go(group, group, pc_s.at[h], pc_r.at[h], {"pix_1": o})
        assemble(h, c)

    def core_gather(h):
        landed(pieces.at[h, o], pc_r.at[h])
        assemble(h, o)

    fetch(0)
    gather_start(0)
    gather_relay(0)
    gather_near(0)
    fetch(1)
    gather_start(1)
    gather_far(0)
    gather_relay(1)
    core_sum(0)
    gather_near(1)
    gather_far(1)
    core_sum(1)
    x_sum(0)
    gone(asked.at[pl.ds(0, 15)], ask_s.at[0])
    gone(cot.at[pl.ds(0, 2 * SIDE)], halo_s.at[0])
    gone(parts, rs.at[0])
    for h in range(2):
        gone(answers.at[h, pl.ds(0, 15)], ans_s.at[h])
        gone(shards.at[h, pl.ds(0, 3)], gs.at[h])
    x_sum(1)
    z_sum(0)
    for h in range(2):
        gone(cs.at[h], core_s.at[h])
        gone(xs.at[h, pl.ds(0, 3)], xs_s.at[h])
    z_sum(1)
    z_gather(0)
    for h in range(2):
        gone(zs.at[h, pl.ds(0, 7)], zs_s.at[h])
    x_gather(0)
    z_gather(1)
    core_gather(0)
    for h in range(2):
        gone(pieces.at[h, 0, 0, pl.ds(0, 7)], pz_s.at[h])
    gone(pieces.at[0, 0, pl.ds(0, 3)], px_s.at[0])
    x_gather(1)
    core_gather(1)
    gone(pieces.at[1, 0, pl.ds(0, 3)], px_s.at[1])
    for h in range(2):
        gone(pieces.at[h, 0], pc_s.at[h])
    for copy in results:
        copy.wait()


def widen_kernel(narrow, wide, held, filled, in_sems, out_sems):
    lines = held.shape[1]
    arriving, leaving = [], []
    for i in range(held.shape[0]):
        rows = pl.ds(i * lines, lines)
        arriving.append(pltpu.make_async_copy(narrow.at[rows], held.at[i], in_sems.at[i]))
        leaving.append(pltpu.make_async_copy(filled.at[i], wide.at[rows], out_sems.at[i]))
        arriving[i].start()
    for i in range(held.shape[0]):
        arriving[i].wait()
        filled[i] = held[i].astype(F32)
        leaving[i].start()
    for copy in leaving:
        copy.wait()


def widened(narrow):
    rows, columns = narrow.shape
    count = 4
    chunk = (count, rows // count, columns)
    anywhere = pl.BlockSpec(memory_space=pl.ANY)
    return pl.pallas_call(
        widen_kernel,
        out_shape=jax.ShapeDtypeStruct(narrow.shape, F32),
        in_specs=[anywhere],
        out_specs=anywhere,
        scratch_shapes=[
            pltpu.VMEM(chunk, BF16),
            pltpu.VMEM(chunk, F32),
            pltpu.SemaphoreType.DMA((count,)),
            pltpu.SemaphoreType.DMA((count,)),
        ],
        name="widen",
    )(narrow)


def shards(spectra, enc_weight, pix_tile, pix_local, foot_weight, cotangent, adjoint, mixing):
    rows, features = spectra.shape[0] // 4, cotangent.shape[1]
    channels = spectra.shape[1]
    dma = pltpu.SemaphoreType.DMA
    anywhere = pl.BlockSpec(memory_space=pl.ANY)
    core, line, wide = channels // 2, channels // 8, channels // 64
    shapes = [
        (enc_weight.shape, BF16),
        ((16, 128), jnp.int32),
        ((16, 128), jnp.int32),
        ((16, 128), F32),
        (adjoint.shape, jnp.int32),
        (mixing.shape, F32),
        (spectra.shape, BF16),
        ((TILE + 256, features), BF16),
        ((2 * TILE + 520, SIDE), F32),
        ((16, SIDE), F32),
        ((8, TILE), jnp.int32),
        ((4 * CAP + 8, SIDE), F32),
        ((4, rows, features), BF16),
        ((4, rows, features), BF16),
        ((2, rows // 2, features), BF16),
        ((16, 1, 128), jnp.int32),
        ((16, 1, 128), jnp.int32),
        None,
        ((rows, 128), F32),
        ((2, 16, CAP, SIDE), BF16),
        ((2, 16, CAP, SIDE), BF16),
        ((rows, features), F32),
        ((rows, 16 * CAP), BF16),
        ((2, rows, SIDE), BF16),
        ((2, 4, rows, SIDE), BF16),
        ((2, SIDE, channels), F32),
        ((2, channels, SIDE), F32),
        ((2, core, SIDE), BF16),
        ((2, core, SIDE), BF16),
        ((2, core, SIDE), F32),
        ((2, 4, line, SIDE), BF16),
        ((2, 4, line, SIDE), BF16),
        ((2, line, SIDE), F32),
        ((2, 8, wide, SIDE), F32),
        ((2, 8, wide, SIDE), BF16),
        ((2, 8, wide, SIDE), BF16),
        ((2, 2, 4, 8, wide, SIDE), BF16),
        ((2, core, SIDE), F32),
        ((2, 2, core, SIDE), BF16),
    ]
    split = shapes.index(None)
    counts = [1, 1, 1, 3, 2, 2, 1, 3, 2, 12, 2, 2, 2, 2, 2, 2, 2, 14, 2, 6, 2, 2]
    encoded = pl.pallas_call(
        whole_kernel,
        out_shape=jax.ShapeDtypeStruct((channels, features), BF16),
        in_specs=[anywhere] * 8,
        out_specs=anywhere,
        scratch_shapes=[pltpu.VMEM(*shape) for shape in shapes[:split]]
        + [pltpu.SMEM((16, 1, 128), jnp.int32), pltpu.SMEM((2, 1, 128), jnp.int32)]
        + [pltpu.SMEM((4, 1, 128), jnp.int32)]
        + [pltpu.SMEM((1, TILE), jnp.int32)] * 8
        + [pltpu.VMEM(*shape) for shape in shapes[split + 1 :]]
        + [dma((4,)), dma(()), dma((8,)), dma(()), dma(()), dma((2,)), dma((6,)), dma((4,))]
        + [dma((n,)) for n in counts],
        compiler_params=pltpu.CompilerParams(collective_id=0, has_side_effects=True),
        name="whole",
    )(
        spectra,
        enc_weight,
        pix_tile.reshape(16, 128),
        pix_local.reshape(16, 128),
        foot_weight.reshape(16, 128),
        cotangent,
        adjoint,
        mixing,
    )
    return widened(encoded)


def solution(mesh):
    finer = Mesh(
        mesh.devices.reshape(mesh.shape["obs"], 8, 2, mesh.shape["chan"]),
        ("obs", "pix_0", "pix_1", "chan"),
    )
    placed = (
        P(OBS_PIX, "chan"),
        P("chan", None),
        P(OBS_PIX, None),
        P(OBS_PIX),
        P(OBS_PIX),
        P(PIX, None),
        P(None, PIX),
        P(),
    )
    return jax.shard_map(
        shards, mesh=finer, in_specs=placed, out_specs=P("chan", None), check_vma=False
    )
```
